32 devices in a mesh: gx: 8 (over z, y), gy: 4 (over x, core).
Axes of the slice: x: 2, y: 2, z: 4, core: 2. Of those that a mesh axis runs over, the one named last changes fastest.
Arguments:
- velocity_u: float32 [16, 512, 512], P(None, 'gx', 'gy'), may hold values from -6 to 6
- velocity_v: float32 [16, 512, 512], P(None, 'gx', 'gy'), may hold values from -6 to 6
- velocity_w: float32 [16, 512, 512], P(None, 'gx', 'gy'), may hold values from -6 to 6
- potential: float32 [16, 512, 512], P(None, 'gx', 'gy'), may hold values from -6 to 6
Outputs:
- lorentz: float32 [3, 16, 512, 512], P(None, None, 'gx', 'gy')
- vorticity: float32 [3, 16, 512, 512], P(None, None, 'gx', 'gy')
- divergence: float32 [16, 512, 512], P(None, 'gx', 'gy')
The draws below stay inside these ranges and needn't reach their ends.
All inputs are finite; a program needn't handle non-finite values.
Results may differ from the reference program's by a relative error of at most 0.00005.
Values sent between devices are 32-bit elements; how exact they have to be, the bound alone decides.
A program may use at most 128 MiB of HBM per device.

```python
import jax
import jax.numpy as jnp
from jax import lax

NZ = 16
NX = 512
NY = 512


def block_levels(stream_key, shape, pieces, low, top_value):
    loudness = 1.0
    for dim, shards_of in pieces:
        heights = jax.random.uniform(jax.random.fold_in(jax.random.fold_in(stream_key, 6), dim), (shards_of,), jnp.float32, low / len(pieces), top_value / len(pieces))
        loudness = loudness * jnp.repeat(jnp.exp(heights), shape[dim] // shards_of).reshape((-1,) + (1,) * (len(shape) - 1 - dim))
    return loudness


def centred(own_key, extent, width, most, split=(), kind=jnp.bfloat16):
    drawn = width * jax.random.normal(own_key, extent, jnp.float32)
    if split:
        drawn = drawn * block_levels(own_key, extent, split, -0.22, 0.18)
    return jnp.clip(drawn, -most, most).astype(kind)


def setup_inputs(seed: int = 0) -> dict:
    key_of = jax.random.split(jax.random.key(seed), 5)
    return {
        "velocity_u": centred(key_of[0], (NZ, NX, NY), 1.0, 6.0, ((1, 8), (2, 4)), jnp.float32),
        "velocity_v": centred(key_of[1], (NZ, NX, NY), 1.0, 6.0, ((1, 8), (2, 4)), jnp.float32),
        "velocity_w": centred(key_of[2], (NZ, NX, NY), 1.0, 6.0, ((1, 8), (2, 4)), jnp.float32),
        "potential": centred(key_of[3], (NZ, NX, NY), 1.0, 6.0, ((1, 8), (2, 4)), jnp.float32),
    }


alpha_inner = 1.0 / 3.0
coef_near = 7.0 / 9.0
coef_far = 1.0 / 36.0
field_bx = 0.6
field_by = 0.8

def z_derivative(field, axis):

    def plus(k):
        return jnp.roll(field, -k, axis) - jnp.roll(field, k, axis)
    return 0.75 * plus(1) - 0.15 * plus(2) + plus(3) / 60.0

def wall_coefficients(rows, total):
    edge = (rows == 1) | (rows == total - 2)
    lower = jnp.where(rows == 0, 0.0, jnp.where(edge, 0.25, jnp.where(rows == total - 1, 2.0, alpha_inner)))
    upper = jnp.where(rows == total - 1, 0.0, jnp.where(edge, 0.25, jnp.where(rows == 0, 2.0, alpha_inner)))
    return (lower.astype(jnp.float32), upper.astype(jnp.float32))

def x_derivative(field):
    count = field.shape[1]
    spectrum = jnp.fft.rfft(field, axis=1)
    theta = 2.0 * jnp.pi * jnp.arange(count // 2 + 1).astype(field.dtype) / count
    symbol = (2.0 * coef_near * jnp.sin(theta) + 2.0 * coef_far * jnp.sin(2.0 * theta)) / (1.0 + 2.0 * alpha_inner * jnp.cos(theta))
    result = jnp.fft.irfft(spectrum * (1j * symbol)[None, :, None], n=count, axis=1)
    return result.astype(field.dtype)

def y_derivative(field):
    total = field.shape[2]
    padded = jnp.pad(field, ((0, 0), (0, 0), (2, 2)))
    right = coef_near * (padded[:, :, 3:-1] - padded[:, :, 1:-3]) + coef_far * (padded[:, :, 4:] - padded[:, :, :-4])
    right = right.at[:, :, 0].set(-2.5 * field[:, :, 0] + 2.0 * field[:, :, 1] + 0.5 * field[:, :, 2])
    right = right.at[:, :, 1].set(0.75 * (field[:, :, 2] - field[:, :, 0]))
    right = right.at[:, :, total - 2].set(0.75 * (field[:, :, total - 1] - field[:, :, total - 3]))
    right = right.at[:, :, total - 1].set(2.5 * field[:, :, total - 1] - 2.0 * field[:, :, total - 2] - 0.5 * field[:, :, total - 3])
    lower, upper = wall_coefficients(jnp.arange(total, dtype=jnp.int32), total)
    diagonal = jnp.ones((total,), field.dtype)
    columns = right.reshape(-1, total).T
    solved = lax.linalg.tridiagonal_solve(lower.astype(field.dtype), diagonal, upper.astype(field.dtype), columns)
    return solved.T.reshape(field.shape)

def assemble(stacked, x_deriv, y_deriv, z_deriv):
    current_x = -x_deriv[3] - field_by * stacked[2]
    current_y = -y_deriv[3] + field_bx * stacked[2]
    current_z = -z_deriv[3] + field_by * stacked[0] - field_bx * stacked[1]
    lorentz = jnp.stack([-field_by * current_z, field_bx * current_z, field_by * current_x - field_bx * current_y])
    vorticity = jnp.stack([y_deriv[2] - z_deriv[1], z_deriv[0] - x_deriv[2], x_deriv[1] - y_deriv[0]])
    divergence = x_deriv[0] + y_deriv[1] + z_deriv[2]
    return (lorentz, vorticity, divergence)

def reference(velocity_u, velocity_v, velocity_w, potential):
    fields = [velocity_u, velocity_v, velocity_w, potential]
    stacked = jnp.stack(fields)
    x_deriv = jnp.stack([x_derivative(f) for f in fields])
    y_deriv = jnp.stack([y_derivative(f) for f in fields])
    z_deriv = z_derivative(stacked, 1)
    lorentz, vorticity, divergence = assemble(stacked, x_deriv, y_deriv, z_deriv)
    return (lorentz, vorticity, divergence)
```

```python
import functools

import jax
import jax.numpy as jnp
import numpy as np
from jax import lax
from jax.experimental import pallas as pl
from jax.experimental.pallas import tpu as pltpu
from jax.sharding import PartitionSpec as P

alpha_inner = 1.0 / 3.0
coef_near = 7.0 / 9.0
coef_far = 1.0 / 36.0
field_bx = 0.6
field_by = 0.8
MESH = pl.DeviceIdType.MESH
f32 = jnp.float32
bf16 = jnp.bfloat16


def np_split(a):
    hi = a.astype(np.float32).astype(bf16)
    lo = (a - hi.astype(np.float64)).astype(np.float32).astype(bf16)
    return hi, lo


def green(offset):
    root = (-1.0 + np.sqrt(1.0 - 4.0 * alpha_inner**2)) / (2.0 * alpha_inner)
    peak = 1.0 / np.sqrt(1.0 - 4.0 * alpha_inner**2)

    def pulse(k):
        return peak * root ** np.abs(k).astype(np.float64)

    near = pulse(offset - 1) - pulse(offset + 1)
    far = pulse(offset - 2) - pulse(offset + 2)
    return coef_near * near + coef_far * far


def x_line(rows):
    i = np.arange(rows)[:, None]
    j = np.arange(-rows, 2 * rows)[None, :]
    whole = green(j - i)
    return whole[:, :rows], whole[:, rows : 2 * rows], whole[:, 2 * rows :]


def y_operator(total):
    t = np.eye(total) + alpha_inner * (np.eye(total, k=1) + np.eye(total, k=-1))
    b = coef_near * (np.eye(total, k=1) - np.eye(total, k=-1))
    b += coef_far * (np.eye(total, k=2) - np.eye(total, k=-2))
    for r, s in ((0, 1), (total - 1, -1)):
        t[r] = 0.0
        b[r] = 0.0
        t[r, r], t[r, r + s] = 1.0, 2.0
        b[r, r], b[r, r + s], b[r, r + 2 * s] = -2.5 * s, 2.0 * s, 0.5 * s
        q = r + s
        t[q] = 0.0
        b[q] = 0.0
        t[q, q - 1], t[q, q], t[q, q + 1] = 0.25, 1.0, 0.25
        b[q, q + 1], b[q, q - 1] = 0.75, -0.75
    return np.linalg.solve(t, b)


def from_left(block):
    v = block[:, -1].copy()
    s = block[1] / block[1, -1]
    v[0] = block[0, -2] / s[-2]
    return v, s, block[0, -1] - v[0]


def from_right(block):
    v, s, gamma = from_left(block[::-1, ::-1])
    return v[::-1], s[::-1], gamma


def x_tables(rows, lanes):
    left, own, right = x_line(rows)
    hi, lo = np_split(own)
    amat = np.concatenate([hi, hi, lo, lo], axis=1)
    vl, sl, gl = from_left(left)
    vr, sr, gr = from_right(right)
    first = np.zeros(rows)
    first[0] = gl
    last = np.zeros(rows)
    last[-1] = gr
    cols = np.stack([vl, vr, sl, sr, first, last])
    return amat, np.repeat(cols[:, :, None], lanes, axis=2).astype(np.float32)


def y_tables(cells, count):
    d = y_operator(cells * count)

    def part(p, q):
        return d[p * cells : (p + 1) * cells, q * cells : (q + 1) * cells]

    mats, sends, backs = [], [], []
    for p in range(count):
        hi, lo = np_split(part(p, p).T)
        mats.append(np.block([[hi, lo], [hi, lo]]))
        send = np.zeros((4, 16, cells))
        back = np.zeros((16, 4, cells))
        for f in range(4):
            if p + 1 < count:
                send[f, 2 * f] = from_left(part(p + 1, p))[1]
                send[f, 2 * f + 1, -1] = 1.0
                v, _, gamma = from_right(part(p, p + 1))
                back[8 + 2 * f, f] = v
                back[8 + 2 * f + 1, f, -1] = gamma
            if p > 0:
                send[f, 8 + 2 * f] = from_right(part(p - 1, p))[1]
                send[f, 8 + 2 * f + 1, 0] = 1.0
                v, _, gamma = from_left(part(p, p - 1))
                back[2 * f, f] = v
                back[2 * f + 1, f, 0] = gamma
        hi, lo = np_split(send)
        rows = np.concatenate([hi, lo], axis=1)
        sends.append(np.concatenate([rows, rows], axis=2))
        hi, lo = np_split(back.reshape(16, 4 * cells))
        backs.append(np.concatenate([hi, hi, lo, lo], axis=0))
    return np.stack(mats), np.stack(sends), np.stack(backs)


def halves(a):
    hi = a.astype(bf16)
    return hi, (a - hi.astype(f32)).astype(bf16)


def dot(a, b, dims=((1,), (0,))):
    return lax.dot_general(a, b, (dims, ((), ())), preferred_element_type=f32)


def kernel(
    u_ref, v_ref, w_ref, p_ref, amat, xcol, ymats, ysends, ybacks,
    lor, vor, div,
    field, ymat, ysend, yback, sendx, recvx, sendy, recvy,
    in_sem, con_sem, sx, rx, sy, ry,
):
    depth, rows, cells = u_ref.shape
    nx, ny = lax.axis_size("gx"), lax.axis_size("gy")
    ix, iy = lax.axis_index("gx"), lax.axis_index("gy")
    right, left = lax.rem(ix + 1, nx), lax.rem(ix + nx - 1, nx)
    up, down = lax.rem(iy + 1, ny), lax.rem(iy + ny - 1, ny)
    has_up, has_down = iy < ny - 1, iy > 0

    loads = [
        pltpu.make_async_copy(src, field.at[k], in_sem.at[k])
        for k, src in enumerate((u_ref, v_ref, w_ref, p_ref))
    ]
    consts = [
        pltpu.make_async_copy(src.at[iy], dst, con_sem.at[k])
        for k, (src, dst) in enumerate(((ysends, ysend), (ymats, ymat), (ybacks, yback)))
    ]
    for c in loads + consts:
        c.start()

    barrier = pltpu.get_barrier_semaphore()
    for other in (left, right):
        pl.semaphore_signal(barrier, inc=1, device_id={"gx": other}, device_id_type=MESH)

    @pl.when(has_up)
    def _():
        pl.semaphore_signal(barrier, inc=1, device_id={"gy": up}, device_id_type=MESH)

    @pl.when(has_down)
    def _():
        pl.semaphore_signal(barrier, inc=1, device_id={"gy": down}, device_id_type=MESH)

    def copy_x(side, k):
        return pltpu.make_async_remote_copy(
            src_ref=sendx.at[side, k], dst_ref=recvx.at[side, k],
            send_sem=sx.at[side, k], recv_sem=rx.at[side, k],
            device_id={"gx": (right, left)[side]}, device_id_type=MESH,
        )

    def copy_y(side):
        return pltpu.make_async_remote_copy(
            src_ref=sendy.at[side], dst_ref=recvy.at[side],
            send_sem=sy.at[side], recv_sem=ry.at[side],
            device_id={"gy": (up, down)[side]}, device_id_type=MESH,
        )

    zeros = jnp.zeros(recvy.shape[1:], f32)

    @pl.when(jnp.logical_not(has_down))
    def _():
        recvy[0] = zeros

    @pl.when(jnp.logical_not(has_up))
    def _():
        recvy[1] = zeros

    for k in range(4):
        loads[k].wait()
        f = field[k]
        sendx[0, k, 0] = jnp.sum(f * xcol[2][None], axis=1)
        sendx[0, k, 1] = field[k, :, rows - 1, :]
        sendx[1, k, 0] = jnp.sum(f * xcol[3][None], axis=1)
        sendx[1, k, 1] = field[k, :, 0, :]
        if k == 0:

            @pl.when(jnp.logical_and(has_up, has_down))
            def _():
                pl.semaphore_wait(barrier, 4)

            @pl.when(jnp.logical_not(jnp.logical_and(has_up, has_down)))
            def _():
                pl.semaphore_wait(barrier, 3)

        for side in range(2):
            copy_x(side, k).start()

    consts[0].wait()
    sums = None
    for k in range(4):
        hi, lo = halves(field[k].reshape(depth * rows, cells))
        part = dot(ysend[k], jnp.concatenate([hi, lo], axis=1), ((1,), (1,)))
        sums = part if sums is None else sums + part
    sums = sums[0:16] + sums[16:32]
    sendy[0] = sums[0:8]
    sendy[1] = sums[8:16]

    @pl.when(has_up)
    def _():
        copy_y(0).start()

    @pl.when(has_down)
    def _():
        copy_y(1).start()

    consts[1].wait()

    def own(z, carry):
        planes = [field[k, z] for k in range(4)]
        split = [halves(a) for a in planes]
        wide = jnp.concatenate([jnp.concatenate(s, axis=1) for s in split], axis=0)
        both = dot(wide, ymat[...])
        dy = both[:, :cells] + both[:, cells:]
        dy = [dy[k * rows : (k + 1) * rows] for k in range(4)]
        tall = jnp.concatenate([jnp.concatenate(s + s, axis=0) for s in split], axis=1)
        dx = dot(amat[...], tall)
        dx = [dx[:, k * cells : (k + 1) * cells] for k in range(4)]

        def at(k, shift):
            return field[k, lax.rem(z + shift + depth, depth)]

        dz = [
            0.75 * (at(k, 1) - at(k, -1))
            - 0.15 * (at(k, 2) - at(k, -2))
            + (1.0 / 60.0) * (at(k, 3) - at(k, -3))
            for k in range(4)
        ]
        u, v, w, _ = planes
        jx = -dx[3] - field_by * w
        jy = -dy[3] + field_bx * w
        jz = -dz[3] + field_by * u - field_bx * v
        lor[0, z] = -field_by * jz
        lor[1, z] = field_bx * jz
        lor[2, z] = field_by * jx - field_bx * jy
        vor[0, z] = dy[2] - dz[1]
        vor[1, z] = dz[0] - dx[2]
        vor[2, z] = dx[1] - dy[0]
        div[z] = dx[0] + dy[1] + dz[2]
        return carry

    lax.fori_loop(0, depth, own, 0)

    consts[2].wait()

    @pl.when(has_up)
    def _():
        copy_y(0).wait_send()
        copy_y(1).wait_recv()

    @pl.when(has_down)
    def _():
        copy_y(1).wait_send()
        copy_y(0).wait_recv()

    for k in range(4):
        for side in range(2):
            copy_x(side, k).wait()

    span = 128 // rows

    def edges(g, carry):
        where = pl.ds(pl.multiple_of(g * 128, 128), 128)
        got = jnp.concatenate([recvy[0, :, where], recvy[1, :, where]], axis=0)
        hi, lo = halves(got)
        ty = dot(jnp.concatenate([hi, lo, hi, lo], axis=0), yback[...], ((0,), (0,)))
        for q in range(span):
            z = g * span + q
            ey = [
                ty[q * rows : (q + 1) * rows, k * cells : (k + 1) * cells] for k in range(4)
            ]
            ex = []
            for k in range(4):
                e = xcol[0] * recvx[0, k, 0, pl.ds(z, 1), :] + xcol[1] * recvx[1, k, 0, pl.ds(z, 1), :]
                top = e[:8] + xcol[4, :8] * recvx[0, k, 1, pl.ds(z, 1), :]
                end = e[rows - 8 :] + xcol[5, rows - 8 :] * recvx[1, k, 1, pl.ds(z, 1), :]
                ex.append(jnp.concatenate([top, e[8 : rows - 8], end], axis=0))
            lor[2, z] += field_bx * ey[3] - field_by * ex[3]
            vor[0, z] += ey[2]
            vor[1, z] -= ex[2]
            vor[2, z] += ex[1] - ey[0]
            div[z] += ex[0] + ey[1]
        return carry

    lax.fori_loop(0, depth // span, edges, 0)


def local(tables, velocity_u, velocity_v, velocity_w, potential):
    depth, rows, cells = velocity_u.shape
    amat, xcol, ymats, ysends, ybacks = tables
    vmem = pl.BlockSpec(memory_space=pltpu.VMEM)
    anywhere = pl.BlockSpec(memory_space=pl.ANY)
    dma = pltpu.SemaphoreType.DMA
    return pl.pallas_call(
        kernel,
        out_shape=(
            jax.ShapeDtypeStruct((3, depth, rows, cells), f32),
            jax.ShapeDtypeStruct((3, depth, rows, cells), f32),
            jax.ShapeDtypeStruct((depth, rows, cells), f32),
        ),
        in_specs=[anywhere] * 4 + [vmem] * 2 + [anywhere] * 3,
        out_specs=[vmem] * 3,
        scratch_shapes=[
            pltpu.VMEM((4, depth, rows, cells), f32),
            pltpu.VMEM(ymats.shape[1:], bf16),
            pltpu.VMEM(ysends.shape[1:], bf16),
            pltpu.VMEM(ybacks.shape[1:], bf16),
            pltpu.VMEM((2, 4, 2, depth, cells), f32),
            pltpu.VMEM((2, 4, 2, depth, cells), f32),
            pltpu.VMEM((2, 8, depth * rows), f32),
            pltpu.VMEM((2, 8, depth * rows), f32),
            dma((4,)),
            dma((3,)),
            dma((2, 4)),
            dma((2, 4)),
            dma((2,)),
            dma((2,)),
        ],
        compiler_params=pltpu.CompilerParams(
            collective_id=0, has_side_effects=True, vmem_limit_bytes=24 * 2**20
        ),
    )(velocity_u, velocity_v, velocity_w, potential, *map(jnp.asarray, tables))


def solution(mesh):
    spec = P(None, "gx", "gy")
    wide = P(None, None, "gx", "gy")

    def whole(velocity_u, velocity_v, velocity_w, potential):
        _, total_x, total_y = velocity_u.shape
        rows, cells = total_x // mesh.shape["gx"], total_y // mesh.shape["gy"]
        tables = x_tables(rows, cells) + y_tables(cells, mesh.shape["gy"])
        return jax.shard_map(
            functools.partial(local, tables),
            mesh=mesh,
            in_specs=(spec,) * 4,
            out_specs=(wide, wide, spec),
            check_vma=False,
        )(velocity_u, velocity_v, velocity_w, potential)

    return whole
```

```python
import functools

import jax
import jax.numpy as jnp
import numpy as np
from jax import lax
from jax.experimental import pallas as pl
from jax.experimental.pallas import tpu as pltpu
from jax.sharding import PartitionSpec as P

alpha_inner = 1.0 / 3.0
coef_near = 7.0 / 9.0
coef_far = 1.0 / 36.0
field_bx = 0.6
field_by = 0.8
MESH = pl.DeviceIdType.MESH
f32 = jnp.float32
bf16 = jnp.bfloat16


def np_split(a):
    hi = a.astype(np.float32).astype(bf16)
    lo = (a - hi.astype(np.float64)).astype(np.float32).astype(bf16)
    return hi, lo


def green(offset):
    root = (-1.0 + np.sqrt(1.0 - 4.0 * alpha_inner**2)) / (2.0 * alpha_inner)
    peak = 1.0 / np.sqrt(1.0 - 4.0 * alpha_inner**2)

    def pulse(k):
        return peak * root ** np.abs(k).astype(np.float64)

    near = pulse(offset - 1) - pulse(offset + 1)
    far = pulse(offset - 2) - pulse(offset + 2)
    return coef_near * near + coef_far * far


def x_line(rows):
    i = np.arange(rows)[:, None]
    j = np.arange(-rows, 2 * rows)[None, :]
    whole = green(j - i)
    return whole[:, :rows], whole[:, rows : 2 * rows], whole[:, 2 * rows :]


def y_operator(total):
    t = np.eye(total) + alpha_inner * (np.eye(total, k=1) + np.eye(total, k=-1))
    b = coef_near * (np.eye(total, k=1) - np.eye(total, k=-1))
    b += coef_far * (np.eye(total, k=2) - np.eye(total, k=-2))
    for r, s in ((0, 1), (total - 1, -1)):
        t[r] = 0.0
        b[r] = 0.0
        t[r, r], t[r, r + s] = 1.0, 2.0
        b[r, r], b[r, r + s], b[r, r + 2 * s] = -2.5 * s, 2.0 * s, 0.5 * s
        q = r + s
        t[q] = 0.0
        b[q] = 0.0
        t[q, q - 1], t[q, q], t[q, q + 1] = 0.25, 1.0, 0.25
        b[q, q + 1], b[q, q - 1] = 0.75, -0.75
    return np.linalg.solve(t, b)


def from_left(block):
    v = block[:, -1].copy()
    s = block[1] / block[1, -1]
    v[0] = block[0, -2] / s[-2]
    return v, s, block[0, -1] - v[0]


def from_right(block):
    v, s, gamma = from_left(block[::-1, ::-1])
    return v[::-1], s[::-1], gamma


def x_tables(rows, lanes):
    left, own, right = x_line(rows)
    hi, lo = np_split(own)
    amat = np.concatenate([hi, hi, lo, lo], axis=1)
    vl, sl, gl = from_left(left)
    vr, sr, gr = from_right(right)
    first = np.zeros(rows)
    first[0] = gl
    last = np.zeros(rows)
    last[-1] = gr
    cols = np.stack([vl, vr, sl, sr, first, last])
    return amat, np.repeat(cols[:, :, None], lanes, axis=2).astype(np.float32)


def y_tables(cells, count):
    d = y_operator(cells * count)

    def part(p, q):
        return d[p * cells : (p + 1) * cells, q * cells : (q + 1) * cells]

    mats, sends, backs = [], [], []
    for p in range(count):
        hi, lo = np_split(part(p, p).T)
        mats.append(np.block([[hi, lo], [hi, lo]]))
        send = np.zeros((4, 16, cells))
        back = np.zeros((16, 4, cells))
        for f in range(4):
            if p + 1 < count:
                send[f, 2 * f] = from_left(part(p + 1, p))[1]
                send[f, 2 * f + 1, -1] = 1.0
                v, _, gamma = from_right(part(p, p + 1))
                back[8 + 2 * f, f] = v
                back[8 + 2 * f + 1, f, -1] = gamma
            if p > 0:
                send[f, 8 + 2 * f] = from_right(part(p - 1, p))[1]
                send[f, 8 + 2 * f + 1, 0] = 1.0
                v, _, gamma = from_left(part(p, p - 1))
                back[2 * f, f] = v
                back[2 * f + 1, f, 0] = gamma
        hi, lo = np_split(send)
        rows = np.concatenate([hi, lo], axis=1)
        sends.append(np.concatenate([rows, rows], axis=2))
        hi, lo = np_split(back.reshape(16, 4 * cells))
        backs.append(np.concatenate([hi, hi, lo, lo], axis=0))
    return np.stack(mats), np.stack(sends), np.stack(backs)


def halves(a):
    hi = a.astype(bf16)
    return hi, (a - hi.astype(f32)).astype(bf16)


def dot(a, b, dims=((1,), (0,))):
    return lax.dot_general(a, b, (dims, ((), ())), preferred_element_type=f32)


def inner_kernel(
    u_ref, v_ref, w_ref, p_ref, amats, xcols, ymats, ysends, ybacks,
    jxy, part, recvx, recvy, xcol, yback,
    field, amat, ymat, ysend, sendx, sendy,
    in_sem, con_sem, sx, rx, sy, ry,
):
    depth, rows, cells = u_ref.shape
    nx, ny = lax.axis_size("gx"), lax.axis_size("gy")
    ix, iy = lax.axis_index("gx"), lax.axis_index("gy")
    right, left = lax.rem(ix + 1, nx), lax.rem(ix + nx - 1, nx)
    up, down = lax.rem(iy + 1, ny), lax.rem(iy + ny - 1, ny)
    has_up, has_down = iy < ny - 1, iy > 0

    loads = [
        pltpu.make_async_copy(src, field.at[k], in_sem.at[k])
        for k, src in enumerate((u_ref, v_ref, w_ref, p_ref))
    ]
    consts = [
        pltpu.make_async_copy(src, dst, con_sem.at[k])
        for k, (src, dst) in enumerate(
            (
                (xcols, xcol),
                (ysends.at[iy], ysend),
                (ymats.at[iy], ymat),
                (amats, amat),
                (ybacks.at[iy], yback),
            )
        )
    ]
    for c in consts[:1] + loads + consts[1:]:
        c.start()

    barrier = pltpu.get_barrier_semaphore()
    for other in (left, right):
        pl.semaphore_signal(barrier, inc=1, device_id={"gx": other}, device_id_type=MESH)

    @pl.when(has_up)
    def _():
        pl.semaphore_signal(barrier, inc=1, device_id={"gy": up}, device_id_type=MESH)

    @pl.when(has_down)
    def _():
        pl.semaphore_signal(barrier, inc=1, device_id={"gy": down}, device_id_type=MESH)

    def copy_x(side, k):
        return pltpu.make_async_remote_copy(
            src_ref=sendx.at[side, k], dst_ref=recvx.at[side, k],
            send_sem=sx.at[side, k], recv_sem=rx.at[side, k],
            device_id={"gx": (right, left)[side]}, device_id_type=MESH,
        )

    def copy_y(side):
        return pltpu.make_async_remote_copy(
            src_ref=sendy.at[side], dst_ref=recvy.at[side],
            send_sem=sy.at[side], recv_sem=ry.at[side],
            device_id={"gy": (up, down)[side]}, device_id_type=MESH,
        )

    zeros = jnp.zeros(recvy.shape[1:], f32)

    @pl.when(jnp.logical_not(has_down))
    def _():
        recvy[0] = zeros

    @pl.when(jnp.logical_not(has_up))
    def _():
        recvy[1] = zeros

    consts[0].wait()
    for k in range(4):
        loads[k].wait()
        f = field[k]
        sendx[0, k, 0] = jnp.sum(f * xcol[2][None], axis=1)
        sendx[0, k, 1] = field[k, :, rows - 1, :]
        sendx[1, k, 0] = jnp.sum(f * xcol[3][None], axis=1)
        sendx[1, k, 1] = field[k, :, 0, :]
        if k == 0:

            @pl.when(jnp.logical_and(has_up, has_down))
            def _():
                pl.semaphore_wait(barrier, 4)

            @pl.when(jnp.logical_not(jnp.logical_and(has_up, has_down)))
            def _():
                pl.semaphore_wait(barrier, 3)

        for side in range(2):
            copy_x(side, k).start()

    consts[1].wait()
    sums = None
    for k in range(4):
        hi, lo = halves(field[k].reshape(depth * rows, cells))
        term = dot(ysend[k], jnp.concatenate([hi, lo], axis=1), ((1,), (1,)))
        sums = term if sums is None else sums + term
    sums = sums[0:16] + sums[16:32]
    sendy[0] = sums[0:8]
    sendy[1] = sums[8:16]

    @pl.when(has_up)
    def _():
        copy_y(0).start()

    @pl.when(has_down)
    def _():
        copy_y(1).start()

    consts[2].wait()
    consts[3].wait()

    def own(z, carry):
        planes = [field[k, z] for k in range(4)]
        split = [halves(a) for a in planes]
        wide = jnp.concatenate([jnp.concatenate(s, axis=1) for s in split], axis=0)
        both = dot(wide, ymat[...])
        dy = both[:, :cells] + both[:, cells:]
        dy = [dy[k * rows : (k + 1) * rows] for k in range(4)]
        tall = jnp.concatenate([jnp.concatenate(s + s, axis=0) for s in split], axis=1)
        dx = dot(amat[...], tall)
        dx = [dx[:, k * cells : (k + 1) * cells] for k in range(4)]

        def at(k, shift):
            return field[k, lax.rem(z + shift + depth, depth)]

        dz = [
            0.75 * (at(k, 1) - at(k, -1))
            - 0.15 * (at(k, 2) - at(k, -2))
            + (1.0 / 60.0) * (at(k, 3) - at(k, -3))
            for k in range(4)
        ]
        u, v, w, _ = planes
        jx = -dx[3] - field_by * w
        jy = -dy[3] + field_bx * w
        jz = -dz[3] + field_by * u - field_bx * v
        jxy[0, z] = -field_by * jz
        jxy[1, z] = field_bx * jz
        part[0, z] = field_by * jx - field_bx * jy
        part[1, z] = dy[2] - dz[1]
        part[2, z] = dz[0] - dx[2]
        part[3, z] = dx[1] - dy[0]
        part[4, z] = dx[0] + dy[1] + dz[2]
        return carry

    lax.fori_loop(0, depth, own, 0)

    consts[4].wait()

    @pl.when(has_up)
    def _():
        copy_y(0).wait_send()
        copy_y(1).wait_recv()

    @pl.when(has_down)
    def _():
        copy_y(1).wait_send()
        copy_y(0).wait_recv()

    for k in range(4):
        for side in range(2):
            copy_x(side, k).wait()


def outer_kernel(jxy, part, recvx, recvy, xcol, yback, lor, vor, div, done, sem):
    _, depth, rows, cells = part.shape
    span = 128 // rows
    through = pltpu.make_async_copy(jxy, lor.at[pl.ds(0, 2)], sem.at[5])
    through.start()
    targets = (lor.at[2], vor.at[0], vor.at[1], vor.at[2], div)

    def edges(g, carry):
        where = pl.ds(pl.multiple_of(g * 128, 128), 128)
        got = jnp.concatenate([recvy[0, :, where], recvy[1, :, where]], axis=0)
        hi, lo = halves(got)
        ty = dot(jnp.concatenate([hi, lo, hi, lo], axis=0), yback[...], ((0,), (0,)))
        for q in range(span):
            z = g * span + q
            ey = [
                ty[q * rows : (q + 1) * rows, k * cells : (k + 1) * cells] for k in range(4)
            ]
            ex = []
            for k in range(4):
                lo_sum, lo_cell, hi_sum, hi_cell = [
                    recvx[side, k, what, pl.ds(z, 1), :] for side in range(2) for what in range(2)
                ]
                e = xcol[0] * lo_sum + xcol[1] * hi_sum
                top = e[:8] + xcol[4, :8] * lo_cell
                end = e[rows - 8 :] + xcol[5, rows - 8 :] * hi_cell
                ex.append(jnp.concatenate([top, e[8 : rows - 8], end], axis=0))
            done[0, z] = part[0, z] + (field_bx * ey[3] - field_by * ex[3])
            done[1, z] = part[1, z] + ey[2]
            done[2, z] = part[2, z] - ex[2]
            done[3, z] = part[3, z] + (ex[1] - ey[0])
            done[4, z] = part[4, z] + (ex[0] + ey[1])
        planes = pl.ds(g * span, span)
        for k in range(5):
            pltpu.make_async_copy(done.at[k, planes], targets[k].at[planes], sem.at[k]).start()
        return carry

    lax.fori_loop(0, depth // span, edges, 0)
    for k in range(5):
        pltpu.make_async_copy(done.at[k], targets[k], sem.at[k]).wait()
    through.wait()


def local(tables, velocity_u, velocity_v, velocity_w, potential):
    depth, rows, cells = velocity_u.shape
    amat, xcol, ymats, ysends, ybacks = tables
    vmem = pl.BlockSpec(memory_space=pltpu.VMEM)
    hbm = pl.BlockSpec(memory_space=pltpu.HBM)
    dma = pltpu.SemaphoreType.DMA

    def shape(*dims, dtype=f32):
        return jax.ShapeDtypeStruct(dims, dtype)

    inner = pl.pallas_call(
        inner_kernel,
        out_shape=(
            shape(2, depth, rows, cells),
            shape(5, depth, rows, cells),
            shape(2, 4, 2, depth, cells),
            shape(2, 8, depth * rows),
            shape(*xcol.shape),
            shape(*ybacks.shape[1:], dtype=bf16),
        ),
        in_specs=[hbm] * 9,
        out_specs=[vmem] * 6,
        scratch_shapes=[
            pltpu.VMEM((4, depth, rows, cells), f32),
            pltpu.VMEM(amat.shape, bf16),
            pltpu.VMEM(ymats.shape[1:], bf16),
            pltpu.VMEM(ysends.shape[1:], bf16),
            pltpu.VMEM((2, 4, 2, depth, cells), f32),
            pltpu.VMEM((2, 8, depth * rows), f32),
            dma((4,)),
            dma((5,)),
            dma((2, 4)),
            dma((2, 4)),
            dma((2,)),
            dma((2,)),
        ],
        compiler_params=pltpu.CompilerParams(
            collective_id=0, has_side_effects=True, vmem_limit_bytes=16 * 2**20
        ),
    )(
        *(
            pltpu.with_memory_space_constraint(a, pltpu.HBM)
            for a in (velocity_u, velocity_v, velocity_w, potential, *map(jnp.asarray, tables))
        )
    )
    return pl.pallas_call(
        outer_kernel,
        out_shape=(
            shape(3, depth, rows, cells),
            shape(3, depth, rows, cells),
            shape(depth, rows, cells),
        ),
        in_specs=[vmem] * 6,
        out_specs=[hbm] * 3,
        scratch_shapes=[pltpu.VMEM((5, depth, rows, cells), f32), dma((6,))],
        compiler_params=pltpu.CompilerParams(vmem_limit_bytes=16 * 2**20),
    )(*inner)


def solution(mesh):
    spec = P(None, "gx", "gy")
    wide = P(None, None, "gx", "gy")

    def whole(velocity_u, velocity_v, velocity_w, potential):
        _, total_x, total_y = velocity_u.shape
        rows, cells = total_x // mesh.shape["gx"], total_y // mesh.shape["gy"]
        tables = x_tables(rows, cells) + y_tables(cells, mesh.shape["gy"])
        return jax.shard_map(
            functools.partial(local, tables),
            mesh=mesh,
            in_specs=(spec,) * 4,
            out_specs=(wide, wide, spec),
            check_vma=False,
        )(velocity_u, velocity_v, velocity_w, potential)

    return whole
```

```python
import functools

import jax
import jax.numpy as jnp
import numpy as np
from jax import lax
from jax.experimental import pallas as pl
from jax.experimental.pallas import tpu as pltpu
from jax.sharding import PartitionSpec as P

alpha_inner = 1.0 / 3.0
coef_near = 7.0 / 9.0
coef_far = 1.0 / 36.0
field_bx = 0.6
field_by = 0.8
MESH = pl.DeviceIdType.MESH
f32 = jnp.float32
bf16 = jnp.bfloat16


def np_split(a):
    hi = a.astype(np.float32).astype(bf16)
    lo = (a - hi.astype(np.float64)).astype(np.float32).astype(bf16)
    return hi, lo


def green(offset):
    root = (-1.0 + np.sqrt(1.0 - 4.0 * alpha_inner**2)) / (2.0 * alpha_inner)
    peak = 1.0 / np.sqrt(1.0 - 4.0 * alpha_inner**2)

    def pulse(k):
        return peak * root ** np.abs(k).astype(np.float64)

    near = pulse(offset - 1) - pulse(offset + 1)
    far = pulse(offset - 2) - pulse(offset + 2)
    return coef_near * near + coef_far * far


def x_line(rows):
    i = np.arange(rows)[:, None]
    j = np.arange(-rows, 2 * rows)[None, :]
    whole = green(j - i)
    return whole[:, :rows], whole[:, rows : 2 * rows], whole[:, 2 * rows :]


def y_operator(total):
    t = np.eye(total) + alpha_inner * (np.eye(total, k=1) + np.eye(total, k=-1))
    b = coef_near * (np.eye(total, k=1) - np.eye(total, k=-1))
    b += coef_far * (np.eye(total, k=2) - np.eye(total, k=-2))
    for r, s in ((0, 1), (total - 1, -1)):
        t[r] = 0.0
        b[r] = 0.0
        t[r, r], t[r, r + s] = 1.0, 2.0
        b[r, r], b[r, r + s], b[r, r + 2 * s] = -2.5 * s, 2.0 * s, 0.5 * s
        q = r + s
        t[q] = 0.0
        b[q] = 0.0
        t[q, q - 1], t[q, q], t[q, q + 1] = 0.25, 1.0, 0.25
        b[q, q + 1], b[q, q - 1] = 0.75, -0.75
    return np.linalg.solve(t, b)


def from_left(block):
    v = block[:, -1].copy()
    s = block[1] / block[1, -1]
    v[0] = block[0, -2] / s[-2]
    return v, s, block[0, -1] - v[0]


def from_right(block):
    v, s, gamma = from_left(block[::-1, ::-1])
    return v[::-1], s[::-1], gamma


def x_tables(rows, lanes):
    left, own, right = x_line(rows)
    hi, lo = np_split(own)
    amat = np.concatenate([hi, hi, lo, lo], axis=1)
    vl, sl, gl = from_left(left)
    vr, sr, gr = from_right(right)
    first = np.zeros(rows)
    first[0] = gl
    last = np.zeros(rows)
    last[-1] = gr
    cols = np.stack([vl, vr, sl, sr, first, last])
    return amat, np.repeat(cols[:, :, None], lanes, axis=2).astype(np.float32)


def y_tables(cells, count):
    d = y_operator(cells * count)

    def part(p, q):
        return d[p * cells : (p + 1) * cells, q * cells : (q + 1) * cells]

    mats, sends, backs = [], [], []
    for p in range(count):
        hi, lo = np_split(part(p, p).T)
        mats.append(np.block([[hi, lo], [hi, lo]]))
        send = np.zeros((4, 16, cells))
        back = np.zeros((16, 4, cells))
        for f in range(4):
            if p + 1 < count:
                send[f, 2 * f] = from_left(part(p + 1, p))[1]
                send[f, 2 * f + 1, -1] = 1.0
                v, _, gamma = from_right(part(p, p + 1))
                back[8 + 2 * f, f] = v
                back[8 + 2 * f + 1, f, -1] = gamma
            if p > 0:
                send[f, 8 + 2 * f] = from_right(part(p - 1, p))[1]
                send[f, 8 + 2 * f + 1, 0] = 1.0
                v, _, gamma = from_left(part(p, p - 1))
                back[2 * f, f] = v
                back[2 * f + 1, f, 0] = gamma
        hi, lo = np_split(send)
        rows = np.concatenate([hi, lo], axis=1)
        sends.append(np.concatenate([rows, rows], axis=2))
        hi, lo = np_split(back.reshape(16, 4 * cells))
        backs.append(np.concatenate([hi, hi, lo, lo], axis=0))
    return np.stack(mats), np.stack(sends), np.stack(backs)


def halves(a):
    hi = a.astype(bf16)
    return hi, (a - hi.astype(f32)).astype(bf16)


def dot(a, b, dims=((1,), (0,))):
    return lax.dot_general(a, b, (dims, ((), ())), preferred_element_type=f32)


def inner_kernel(
    u_ref, v_ref, w_ref, p_ref, amats, xcols, ymats, ysends, ybacks,
    ready, part, recvx, xcol,
    field, amat, ymat, ysend, yback, wsum, sendx, sendy, recvy,
    in_sem, con_sem, sx, rx, sy, ry,
):
    depth, rows, cells = u_ref.shape
    nx, ny = lax.axis_size("gx"), lax.axis_size("gy")
    ix, iy = lax.axis_index("gx"), lax.axis_index("gy")
    right, left = lax.rem(ix + 1, nx), lax.rem(ix + nx - 1, nx)
    up, down = lax.rem(iy + 1, ny), lax.rem(iy + ny - 1, ny)
    has_up, has_down = iy < ny - 1, iy > 0

    loads = [
        pltpu.make_async_copy(src, field.at[k], in_sem.at[k])
        for k, src in enumerate((u_ref, v_ref, w_ref, p_ref))
    ]
    consts = [
        pltpu.make_async_copy(src, dst, con_sem.at[k])
        for k, (src, dst) in enumerate(
            (
                (xcols.at[pl.ds(2, 2)], wsum),
                (ysends.at[iy], ysend),
                (ymats.at[iy], ymat),
                (amats, amat),
                (ybacks.at[iy], yback),
                (xcols, xcol),
            )
        )
    ]
    for c in consts[:1] + loads + consts[1:]:
        c.start()

    barrier = pltpu.get_barrier_semaphore()
    for other in (left, right):
        pl.semaphore_signal(barrier, inc=1, device_id={"gx": other}, device_id_type=MESH)

    @pl.when(has_up)
    def _():
        pl.semaphore_signal(barrier, inc=1, device_id={"gy": up}, device_id_type=MESH)

    @pl.when(has_down)
    def _():
        pl.semaphore_signal(barrier, inc=1, device_id={"gy": down}, device_id_type=MESH)

    def copy_x(side, k):
        return pltpu.make_async_remote_copy(
            src_ref=sendx.at[side, k], dst_ref=recvx.at[side, k],
            send_sem=sx.at[side, k], recv_sem=rx.at[side, k],
            device_id={"gx": (right, left)[side]}, device_id_type=MESH,
        )

    def copy_y(side):
        return pltpu.make_async_remote_copy(
            src_ref=sendy.at[side], dst_ref=recvy.at[side],
            send_sem=sy.at[side], recv_sem=ry.at[side],
            device_id={"gy": (up, down)[side]}, device_id_type=MESH,
        )

    zeros = jnp.zeros(recvy.shape[1:], f32)

    @pl.when(jnp.logical_not(has_down))
    def _():
        recvy[0] = zeros

    @pl.when(jnp.logical_not(has_up))
    def _():
        recvy[1] = zeros

    consts[0].wait()
    for side in range(2):
        weight = wsum[side][None]
        for k in range(4):
            if side == 0:
                loads[k].wait()
            sendx[side, k, 0] = jnp.sum(field[k] * weight, axis=1)
            sendx[side, k, 1] = field[k, :, (rows - 1, 0)[side], :]
            if side == 0 and k == 0:

                @pl.when(jnp.logical_and(has_up, has_down))
                def _():
                    pl.semaphore_wait(barrier, 4)

                @pl.when(jnp.logical_not(jnp.logical_and(has_up, has_down)))
                def _():
                    pl.semaphore_wait(barrier, 3)

            copy_x(side, k).start()

    consts[1].wait()
    sums = None
    for k in range(4):
        hi, lo = halves(field[k].reshape(depth * rows, cells))
        term = dot(ysend[k], jnp.concatenate([hi, lo], axis=1), ((1,), (1,)))
        sums = term if sums is None else sums + term
    sums = sums[0:16] + sums[16:32]
    sendy[0] = sums[0:8]
    sendy[1] = sums[8:16]

    @pl.when(has_up)
    def _():
        copy_y(0).start()

    @pl.when(has_down)
    def _():
        copy_y(1).start()

    consts[2].wait()
    consts[3].wait()

    def own(z, carry):
        planes = [field[k, z] for k in range(4)]
        split = [halves(a) for a in planes]
        wide = jnp.concatenate([jnp.concatenate(s, axis=1) for s in split], axis=0)
        both = dot(wide, ymat[...])
        dy = both[:, :cells] + both[:, cells:]
        dy = [dy[k * rows : (k + 1) * rows] for k in range(4)]
        tall = jnp.concatenate([jnp.concatenate(s + s, axis=0) for s in split], axis=1)
        dx = dot(amat[...], tall)
        dx = [dx[:, k * cells : (k + 1) * cells] for k in range(4)]

        def at(k, shift):
            return field[k, lax.rem(z + shift + depth, depth)]

        dz = [
            0.75 * (at(k, 1) - at(k, -1))
            - 0.15 * (at(k, 2) - at(k, -2))
            + (1.0 / 60.0) * (at(k, 3) - at(k, -3))
            for k in range(4)
        ]
        u, v, w, _ = planes
        jx = -dx[3] - field_by * w
        jy = -dy[3] + field_bx * w
        jz = -dz[3] + field_by * u - field_bx * v
        ready[0, z] = -field_by * jz
        ready[1, z] = field_bx * jz
        ready[2, z] = dy[2] - dz[1]
        part[0, z] = field_by * jx - field_bx * jy
        part[1, z] = dz[0] - dx[2]
        part[2, z] = dx[1] - dy[0]
        part[3, z] = dx[0] + dy[1] + dz[2]
        return carry

    lax.fori_loop(0, depth, own, 0)

    consts[4].wait()

    @pl.when(has_up)
    def _():
        copy_y(0).wait_send()
        copy_y(1).wait_recv()

    @pl.when(has_down)
    def _():
        copy_y(1).wait_send()
        copy_y(0).wait_recv()

    span = 128 // rows

    def edges(g, carry):
        where = pl.ds(pl.multiple_of(g * 128, 128), 128)
        got = jnp.concatenate([recvy[0, :, where], recvy[1, :, where]], axis=0)
        hi, lo = halves(got)
        ty = dot(jnp.concatenate([hi, lo, hi, lo], axis=0), yback[...], ((0,), (0,)))
        for q in range(span):
            z = g * span + q
            ey = [
                ty[q * rows : (q + 1) * rows, k * cells : (k + 1) * cells] for k in range(4)
            ]
            ready[2, z] += ey[2]
            part[0, z] += field_bx * ey[3]
            part[2, z] -= ey[0]
            part[3, z] += ey[1]
        return carry

    lax.fori_loop(0, depth // span, edges, 0)
    consts[5].wait()
    for side in range(2):
        for k in range(4):
            copy_x(side, k).wait()


def outer_kernel(ready, part, recvx, xcol, lor, vor, div, done, sem):
    _, depth, rows, cells = part.shape
    through = [
        pltpu.make_async_copy(ready.at[pl.ds(0, 2)], lor.at[pl.ds(0, 2)], sem.at[4]),
        pltpu.make_async_copy(ready.at[2], vor.at[0], sem.at[5]),
    ]
    for c in through:
        c.start()
    plan = (
        (lor.at[2], 3, -field_by),
        (vor.at[1], 2, -1.0),
        (vor.at[2], 1, 1.0),
        (div, 0, 1.0),
    )
    span = 2

    def edges(g, carry):
        planes = pl.ds(g * span, span)
        for a, (target, k, factor) in enumerate(plan):
            for q in range(span):
                z = g * span + q
                lo_sum, lo_cell, hi_sum, hi_cell = [
                    factor * recvx[side, k, what, pl.ds(z, 1), :]
                    for side in range(2)
                    for what in range(2)
                ]
                e = part[a, z] + xcol[0] * lo_sum + xcol[1] * hi_sum
                top = e[:8] + xcol[4, :8] * lo_cell
                end = e[rows - 8 :] + xcol[5, rows - 8 :] * hi_cell
                done[a, z] = jnp.concatenate([top, e[8 : rows - 8], end], axis=0)
            pltpu.make_async_copy(done.at[a, planes], target.at[planes], sem.at[a]).start()
        return carry

    lax.fori_loop(0, depth // span, edges, 0)
    for a, (target, _, _) in enumerate(plan):
        pltpu.make_async_copy(done.at[a], target, sem.at[a]).wait()
    for c in through:
        c.wait()


def local(tables, velocity_u, velocity_v, velocity_w, potential):
    depth, rows, cells = velocity_u.shape
    amat, xcol, ymats, ysends, ybacks = tables
    vmem = pl.BlockSpec(memory_space=pltpu.VMEM)
    hbm = pl.BlockSpec(memory_space=pltpu.HBM)
    dma = pltpu.SemaphoreType.DMA

    def shape(*dims, dtype=f32):
        return jax.ShapeDtypeStruct(dims, dtype)

    inner = pl.pallas_call(
        inner_kernel,
        out_shape=(
            shape(3, depth, rows, cells),
            shape(4, depth, rows, cells),
            shape(2, 4, 2, depth, cells),
            shape(*xcol.shape),
        ),
        in_specs=[hbm] * 9,
        out_specs=[vmem] * 4,
        scratch_shapes=[
            pltpu.VMEM((4, depth, rows, cells), f32),
            pltpu.VMEM(amat.shape, bf16),
            pltpu.VMEM(ymats.shape[1:], bf16),
            pltpu.VMEM(ysends.shape[1:], bf16),
            pltpu.VMEM(ybacks.shape[1:], bf16),
            pltpu.VMEM((2, rows, cells), f32),
            pltpu.VMEM((2, 4, 2, depth, cells), f32),
            pltpu.VMEM((2, 8, depth * rows), f32),
            pltpu.VMEM((2, 8, depth * rows), f32),
            dma((4,)),
            dma((6,)),
            dma((2, 4)),
            dma((2, 4)),
            dma((2,)),
            dma((2,)),
        ],
        compiler_params=pltpu.CompilerParams(
            collective_id=0, has_side_effects=True, vmem_limit_bytes=16 * 2**20
        ),
    )(
        *(
            pltpu.with_memory_space_constraint(a, pltpu.HBM)
            for a in (velocity_u, velocity_v, velocity_w, potential, *map(jnp.asarray, tables))
        )
    )
    return pl.pallas_call(
        outer_kernel,
        out_shape=(
            shape(3, depth, rows, cells),
            shape(3, depth, rows, cells),
            shape(depth, rows, cells),
        ),
        in_specs=[vmem] * 4,
        out_specs=[hbm] * 3,
        scratch_shapes=[pltpu.VMEM((4, depth, rows, cells), f32), dma((6,))],
        compiler_params=pltpu.CompilerParams(vmem_limit_bytes=16 * 2**20),
    )(*inner)


def solution(mesh):
    spec = P(None, "gx", "gy")
    wide = P(None, None, "gx", "gy")

    def whole(velocity_u, velocity_v, velocity_w, potential):
        _, total_x, total_y = velocity_u.shape
        rows, cells = total_x // mesh.shape["gx"], total_y // mesh.shape["gy"]
        tables = x_tables(rows, cells) + y_tables(cells, mesh.shape["gy"])
        return jax.shard_map(
            functools.partial(local, tables),
            mesh=mesh,
            in_specs=(spec,) * 4,
            out_specs=(wide, wide, spec),
            check_vma=False,
        )(velocity_u, velocity_v, velocity_w, potential)

    return whole
```

```python
import functools

import jax
import jax.numpy as jnp
import numpy as np
from jax import lax
from jax.experimental import pallas as pl
from jax.experimental.pallas import tpu as pltpu
from jax.sharding import PartitionSpec as P

alpha_inner = 1.0 / 3.0
coef_near = 7.0 / 9.0
coef_far = 1.0 / 36.0
field_bx = 0.6
field_by = 0.8
MESH = pl.DeviceIdType.MESH
f32 = jnp.float32
bf16 = jnp.bfloat16


def np_split(a):
    hi = a.astype(np.float32).astype(bf16)
    lo = (a - hi.astype(np.float64)).astype(np.float32).astype(bf16)
    return hi, lo


def green(offset):
    root = (-1.0 + np.sqrt(1.0 - 4.0 * alpha_inner**2)) / (2.0 * alpha_inner)
    peak = 1.0 / np.sqrt(1.0 - 4.0 * alpha_inner**2)

    def pulse(k):
        return peak * root ** np.abs(k).astype(np.float64)

    near = pulse(offset - 1) - pulse(offset + 1)
    far = pulse(offset - 2) - pulse(offset + 2)
    return coef_near * near + coef_far * far


def x_line(rows):
    i = np.arange(rows)[:, None]
    j = np.arange(-rows, 2 * rows)[None, :]
    whole = green(j - i)
    return whole[:, :rows], whole[:, rows : 2 * rows], whole[:, 2 * rows :]


def y_operator(total):
    t = np.eye(total) + alpha_inner * (np.eye(total, k=1) + np.eye(total, k=-1))
    b = coef_near * (np.eye(total, k=1) - np.eye(total, k=-1))
    b += coef_far * (np.eye(total, k=2) - np.eye(total, k=-2))
    for r, s in ((0, 1), (total - 1, -1)):
        t[r] = 0.0
        b[r] = 0.0
        t[r, r], t[r, r + s] = 1.0, 2.0
        b[r, r], b[r, r + s], b[r, r + 2 * s] = -2.5 * s, 2.0 * s, 0.5 * s
        q = r + s
        t[q] = 0.0
        b[q] = 0.0
        t[q, q - 1], t[q, q], t[q, q + 1] = 0.25, 1.0, 0.25
        b[q, q + 1], b[q, q - 1] = 0.75, -0.75
    return np.linalg.solve(t, b)


def from_left(block):
    v = block[:, -1].copy()
    s = block[1] / block[1, -1]
    v[0] = block[0, -2] / s[-2]
    return v, s, block[0, -1] - v[0]


def from_right(block):
    v, s, gamma = from_left(block[::-1, ::-1])
    return v[::-1], s[::-1], gamma


def x_tables(rows, lanes):
    left, own, right = x_line(rows)
    hi, lo = np_split(own)
    amat = np.concatenate([hi, hi, lo, lo], axis=1)
    vl, sl, gl = from_left(left)
    vr, sr, gr = from_right(right)
    first = np.zeros(rows)
    first[0] = gl
    last = np.zeros(rows)
    last[-1] = gr
    cols = np.stack([vl, vr, sl, sr, first, last])
    return amat, np.repeat(cols[:, :, None], lanes, axis=2).astype(np.float32)


def y_tables(cells, count):
    d = y_operator(cells * count)

    def part(p, q):
        return d[p * cells : (p + 1) * cells, q * cells : (q + 1) * cells]

    mats, sends, backs = [], [], []
    for p in range(count):
        hi, lo = np_split(part(p, p).T)
        mats.append(np.block([[hi, lo], [hi, lo]]))
        send = np.zeros((4, 16, cells))
        back = np.zeros((16, 4, cells))
        for f in range(4):
            if p + 1 < count:
                send[f, 2 * f] = from_left(part(p + 1, p))[1]
                send[f, 2 * f + 1, -1] = 1.0
                v, _, gamma = from_right(part(p, p + 1))
                back[8 + 2 * f, f] = v
                back[8 + 2 * f + 1, f, -1] = gamma
            if p > 0:
                send[f, 8 + 2 * f] = from_right(part(p - 1, p))[1]
                send[f, 8 + 2 * f + 1, 0] = 1.0
                v, _, gamma = from_left(part(p, p - 1))
                back[2 * f, f] = v
                back[2 * f + 1, f, 0] = gamma
        hi, lo = np_split(send)
        rows = np.concatenate([hi, lo], axis=1)
        sends.append(np.concatenate([rows, rows], axis=2))
        hi, lo = np_split(back.reshape(16, 4 * cells))
        backs.append(np.concatenate([hi, hi, lo, lo], axis=0))
    return np.stack(mats), np.stack(sends), np.stack(backs)


def halves(a):
    hi = a.astype(bf16)
    return hi, (a - hi.astype(f32)).astype(bf16)


def dot(a, b, dims=((1,), (0,))):
    return lax.dot_general(a, b, (dims, ((), ())), preferred_element_type=f32)


def inner_kernel(
    u_ref, v_ref, w_ref, p_ref, amats, xcols, ymats, ysends, ybacks,
    ready, part, recvx, xcol,
    field, amat, ymat, ysend, yback, wsum, sendx, sendy, recvy,
    in_sem, con_sem, sx, rx, sy, ry,
):
    depth, rows, cells = u_ref.shape
    nx, ny = lax.axis_size("gx"), lax.axis_size("gy")
    ix, iy = lax.axis_index("gx"), lax.axis_index("gy")
    right, left = lax.rem(ix + 1, nx), lax.rem(ix + nx - 1, nx)
    up, down = lax.rem(iy + 1, ny), lax.rem(iy + ny - 1, ny)
    has_up, has_down = iy < ny - 1, iy > 0

    loads = [
        pltpu.make_async_copy(src, field.at[k], in_sem.at[k])
        for k, src in enumerate((u_ref, v_ref, w_ref, p_ref))
    ]
    consts = [
        pltpu.make_async_copy(src, dst, con_sem.at[k])
        for k, (src, dst) in enumerate(
            (
                (xcols.at[pl.ds(2, 2)], wsum),
                (ysends.at[iy], ysend),
                (ymats.at[iy], ymat),
                (amats, amat),
                (ybacks.at[iy], yback),
                (xcols, xcol),
            )
        )
    ]
    for c in consts[:1] + loads + consts[1:]:
        c.start()

    barrier = pltpu.get_barrier_semaphore()
    for other in (left, right):
        pl.semaphore_signal(barrier, inc=1, device_id={"gx": other}, device_id_type=MESH)

    @pl.when(has_up)
    def _():
        pl.semaphore_signal(barrier, inc=1, device_id={"gy": up}, device_id_type=MESH)

    @pl.when(has_down)
    def _():
        pl.semaphore_signal(barrier, inc=1, device_id={"gy": down}, device_id_type=MESH)

    def copy_x(side, k):
        return pltpu.make_async_remote_copy(
            src_ref=sendx.at[side, k], dst_ref=recvx.at[side, k],
            send_sem=sx.at[side, k], recv_sem=rx.at[side, k],
            device_id={"gx": (right, left)[side]}, device_id_type=MESH,
        )

    def copy_y(side):
        return pltpu.make_async_remote_copy(
            src_ref=sendy.at[side], dst_ref=recvy.at[side],
            send_sem=sy.at[side], recv_sem=ry.at[side],
            device_id={"gy": (up, down)[side]}, device_id_type=MESH,
        )

    zeros = jnp.zeros(recvy.shape[1:], f32)

    @pl.when(jnp.logical_not(has_down))
    def _():
        recvy[0] = zeros

    @pl.when(jnp.logical_not(has_up))
    def _():
        recvy[1] = zeros

    def enter():
        inside = jnp.logical_and(has_up, has_down)

        @pl.when(inside)
        def _():
            pl.semaphore_wait(barrier, 4)

        @pl.when(jnp.logical_not(inside))
        def _():
            pl.semaphore_wait(barrier, 3)

    def sum_x(side, k):
        sendx[side, k, 0] = jnp.sum(field[k] * wsum[side][None], axis=1)
        sendx[side, k, 1] = field[k, :, (rows - 1, 0)[side], :]

    def sum_y():
        consts[1].wait()
        sums = None
        for k in range(4):
            hi, lo = halves(field[k].reshape(depth * rows, cells))
            term = dot(ysend[k], jnp.concatenate([hi, lo], axis=1), ((1,), (1,)))
            sums = term if sums is None else sums + term
        sums = sums[0:16] + sums[16:32]
        sendy[0] = sums[0:8]
        sendy[1] = sums[8:16]

    def send_y():
        @pl.when(has_up)
        def _():
            copy_y(0).start()

        @pl.when(has_down)
        def _():
            copy_y(1).start()

    def own(z, carry):
        planes = [field[k, z] for k in range(4)]
        split = [halves(a) for a in planes]
        wide = jnp.concatenate([jnp.concatenate(s, axis=1) for s in split], axis=0)
        both = dot(wide, ymat[...])
        dy = both[:, :cells] + both[:, cells:]
        dy = [dy[k * rows : (k + 1) * rows] for k in range(4)]
        tall = jnp.concatenate([jnp.concatenate(s + s, axis=0) for s in split], axis=1)
        dx = dot(amat[...], tall)
        dx = [dx[:, k * cells : (k + 1) * cells] for k in range(4)]

        def at(k, shift):
            return field[k, lax.rem(z + shift + depth, depth)]

        dz = [
            0.75 * (at(k, 1) - at(k, -1))
            - 0.15 * (at(k, 2) - at(k, -2))
            + (1.0 / 60.0) * (at(k, 3) - at(k, -3))
            for k in range(4)
        ]
        u, v, w, _ = planes
        jx = -dx[3] - field_by * w
        jy = -dy[3] + field_bx * w
        jz = -dz[3] + field_by * u - field_bx * v
        ready[0, z] = -field_by * jz
        ready[1, z] = field_bx * jz
        ready[2, z] = dy[2] - dz[1]
        part[0, z] = field_by * jx - field_bx * jy
        part[1, z] = dz[0] - dx[2]
        part[2, z] = dx[1] - dy[0]
        part[3, z] = dx[0] + dy[1] + dz[2]
        return carry

    def compute():
        consts[2].wait()
        consts[3].wait()
        lax.fori_loop(0, depth, own, 0, unroll=2)

    consts[0].wait()

    @pl.when(ix == 0)
    def _():
        for k in range(4):
            loads[k].wait()
            for side in range(2):
                sum_x(side, k)
        sum_y()
        compute()
        enter()
        for side in (1, 0):
            for k in range(4):
                copy_x(side, k).start()
        send_y()

    @pl.when(ix != 0)
    def _():
        for side in range(2):
            for k in range(4):
                if side == 0:
                    loads[k].wait()
                sum_x(side, k)
                if side == 0 and k == 0:
                    enter()
                copy_x(side, k).start()
        sum_y()
        send_y()
        compute()

    consts[4].wait()

    @pl.when(has_up)
    def _():
        copy_y(0).wait_send()
        copy_y(1).wait_recv()

    @pl.when(has_down)
    def _():
        copy_y(1).wait_send()
        copy_y(0).wait_recv()

    span = 128 // rows

    def edges(g, carry):
        where = pl.ds(pl.multiple_of(g * 128, 128), 128)
        got = jnp.concatenate([recvy[0, :, where], recvy[1, :, where]], axis=0)
        hi, lo = halves(got)
        ty = dot(jnp.concatenate([hi, lo, hi, lo], axis=0), yback[...], ((0,), (0,)))
        for q in range(span):
            z = g * span + q
            ey = [
                ty[q * rows : (q + 1) * rows, k * cells : (k + 1) * cells] for k in range(4)
            ]
            ready[2, z] += ey[2]
            part[0, z] += field_bx * ey[3]
            part[2, z] -= ey[0]
            part[3, z] += ey[1]
        return carry

    lax.fori_loop(0, depth // span, edges, 0, unroll=4)
    consts[5].wait()
    for side in range(2):
        for k in range(4):
            copy_x(side, k).wait()


def outer_kernel(ready, part, recvx, xcol, lor, vor, div, done, sem):
    _, depth, rows, cells = part.shape
    through = [
        pltpu.make_async_copy(ready.at[pl.ds(0, 2)], lor.at[pl.ds(0, 2)], sem.at[4]),
        pltpu.make_async_copy(ready.at[2], vor.at[0], sem.at[5]),
    ]
    for c in through:
        c.start()
    plan = (
        (lor.at[2], 3, -field_by),
        (vor.at[1], 2, -1.0),
        (vor.at[2], 1, 1.0),
        (div, 0, 1.0),
    )
    span = 2

    def edges(g, carry):
        planes = pl.ds(g * span, span)
        for a, (target, k, factor) in enumerate(plan):
            for q in range(span):
                z = g * span + q
                lo_sum, lo_cell, hi_sum, hi_cell = [
                    factor * recvx[side, k, what, pl.ds(z, 1), :]
                    for side in range(2)
                    for what in range(2)
                ]
                e = part[a, z] + xcol[0] * lo_sum + xcol[1] * hi_sum
                top = e[:8] + xcol[4, :8] * lo_cell
                end = e[rows - 8 :] + xcol[5, rows - 8 :] * hi_cell
                done[a, z] = jnp.concatenate([top, e[8 : rows - 8], end], axis=0)
            pltpu.make_async_copy(done.at[a, planes], target.at[planes], sem.at[a]).start()
        return carry

    lax.fori_loop(0, depth // span, edges, 0)
    for a, (target, _, _) in enumerate(plan):
        pltpu.make_async_copy(done.at[a], target, sem.at[a]).wait()
    for c in through:
        c.wait()


def local(tables, velocity_u, velocity_v, velocity_w, potential):
    depth, rows, cells = velocity_u.shape
    amat, xcol, ymats, ysends, ybacks = tables
    vmem = pl.BlockSpec(memory_space=pltpu.VMEM)
    hbm = pl.BlockSpec(memory_space=pltpu.HBM)
    dma = pltpu.SemaphoreType.DMA

    def shape(*dims, dtype=f32):
        return jax.ShapeDtypeStruct(dims, dtype)

    inner = pl.pallas_call(
        inner_kernel,
        out_shape=(
            shape(3, depth, rows, cells),
            shape(4, depth, rows, cells),
            shape(2, 4, 2, depth, cells),
            shape(*xcol.shape),
        ),
        in_specs=[hbm] * 9,
        out_specs=[vmem] * 4,
        scratch_shapes=[
            pltpu.VMEM((4, depth, rows, cells), f32),
            pltpu.VMEM(amat.shape, bf16),
            pltpu.VMEM(ymats.shape[1:], bf16),
            pltpu.VMEM(ysends.shape[1:], bf16),
            pltpu.VMEM(ybacks.shape[1:], bf16),
            pltpu.VMEM((2, rows, cells), f32),
            pltpu.VMEM((2, 4, 2, depth, cells), f32),
            pltpu.VMEM((2, 8, depth * rows), f32),
            pltpu.VMEM((2, 8, depth * rows), f32),
            dma((4,)),
            dma((6,)),
            dma((2, 4)),
            dma((2, 4)),
            dma((2,)),
            dma((2,)),
        ],
        compiler_params=pltpu.CompilerParams(
            collective_id=0, has_side_effects=True, vmem_limit_bytes=16 * 2**20
        ),
    )(
        *(
            pltpu.with_memory_space_constraint(a, pltpu.HBM)
            for a in (velocity_u, velocity_v, velocity_w, potential, *map(jnp.asarray, tables))
        )
    )
    return pl.pallas_call(
        outer_kernel,
        out_shape=(
            shape(3, depth, rows, cells),
            shape(3, depth, rows, cells),
            shape(depth, rows, cells),
        ),
        in_specs=[vmem] * 4,
        out_specs=[hbm] * 3,
        scratch_shapes=[pltpu.VMEM((4, depth, rows, cells), f32), dma((6,))],
        compiler_params=pltpu.CompilerParams(vmem_limit_bytes=16 * 2**20),
    )(*inner)


def solution(mesh):
    spec = P(None, "gx", "gy")
    wide = P(None, None, "gx", "gy")

    def whole(velocity_u, velocity_v, velocity_w, potential):
        _, total_x, total_y = velocity_u.shape
        rows, cells = total_x // mesh.shape["gx"], total_y // mesh.shape["gy"]
        tables = x_tables(rows, cells) + y_tables(cells, mesh.shape["gy"])
        return jax.shard_map(
            functools.partial(local, tables),
            mesh=mesh,
            in_specs=(spec,) * 4,
            out_specs=(wide, wide, spec),
            check_vma=False,
        )(velocity_u, velocity_v, velocity_w, potential)

    return whole
```

```python
import functools

import jax
import jax.numpy as jnp
import numpy as np
from jax import lax
from jax.experimental import pallas as pl
from jax.experimental.pallas import tpu as pltpu
from jax.sharding import PartitionSpec as P

alpha_inner = 1.0 / 3.0
coef_near = 7.0 / 9.0
coef_far = 1.0 / 36.0
field_bx = 0.6
field_by = 0.8
MESH = pl.DeviceIdType.MESH
f32 = jnp.float32
bf16 = jnp.bfloat16


def np_split(a):
    hi = a.astype(np.float32).astype(bf16)
    lo = (a - hi.astype(np.float64)).astype(np.float32).astype(bf16)
    return hi, lo


def green(offset):
    root = (-1.0 + np.sqrt(1.0 - 4.0 * alpha_inner**2)) / (2.0 * alpha_inner)
    peak = 1.0 / np.sqrt(1.0 - 4.0 * alpha_inner**2)

    def pulse(k):
        return peak * root ** np.abs(k).astype(np.float64)

    near = pulse(offset - 1) - pulse(offset + 1)
    far = pulse(offset - 2) - pulse(offset + 2)
    return coef_near * near + coef_far * far


def x_line(rows):
    i = np.arange(rows)[:, None]
    j = np.arange(-rows, 2 * rows)[None, :]
    whole = green(j - i)
    return whole[:, :rows], whole[:, rows : 2 * rows], whole[:, 2 * rows :]


def y_operator(total):
    t = np.eye(total) + alpha_inner * (np.eye(total, k=1) + np.eye(total, k=-1))
    b = coef_near * (np.eye(total, k=1) - np.eye(total, k=-1))
    b += coef_far * (np.eye(total, k=2) - np.eye(total, k=-2))
    for r, s in ((0, 1), (total - 1, -1)):
        t[r] = 0.0
        b[r] = 0.0
        t[r, r], t[r, r + s] = 1.0, 2.0
        b[r, r], b[r, r + s], b[r, r + 2 * s] = -2.5 * s, 2.0 * s, 0.5 * s
        q = r + s
        t[q] = 0.0
        b[q] = 0.0
        t[q, q - 1], t[q, q], t[q, q + 1] = 0.25, 1.0, 0.25
        b[q, q + 1], b[q, q - 1] = 0.75, -0.75
    return np.linalg.solve(t, b)


def from_left(block):
    v = block[:, -1].copy()
    s = block[1] / block[1, -1]
    v[0] = block[0, -2] / s[-2]
    return v, s, block[0, -1] - v[0]


def from_right(block):
    v, s, gamma = from_left(block[::-1, ::-1])
    return v[::-1], s[::-1], gamma


def x_tables(rows, lanes):
    left, own, right = x_line(rows)
    hi, lo = np_split(own)
    amat = np.concatenate([hi, hi, lo, lo], axis=1)
    vl, sl, gl = from_left(left)
    vr, sr, gr = from_right(right)
    first = np.zeros(rows)
    first[0] = gl
    last = np.zeros(rows)
    last[-1] = gr
    cols = np.stack([vl, vr, sl, sr, first, last])
    return amat, np.repeat(cols[:, :, None], lanes, axis=2).astype(np.float32)


def y_tables(cells, count):
    d = y_operator(cells * count)

    def part(p, q):
        return d[p * cells : (p + 1) * cells, q * cells : (q + 1) * cells]

    mats, sends, backs = [], [], []
    for p in range(count):
        hi, lo = np_split(part(p, p).T)
        mats.append(np.block([[hi, lo], [hi, lo]]))
        send = np.zeros((4, 16, cells))
        back = np.zeros((16, 4, cells))
        for f in range(4):
            if p + 1 < count:
                send[f, 2 * f] = from_left(part(p + 1, p))[1]
                send[f, 2 * f + 1, -1] = 1.0
                v, _, gamma = from_right(part(p, p + 1))
                back[8 + 2 * f, f] = v
                back[8 + 2 * f + 1, f, -1] = gamma
            if p > 0:
                send[f, 8 + 2 * f] = from_right(part(p - 1, p))[1]
                send[f, 8 + 2 * f + 1, 0] = 1.0
                v, _, gamma = from_left(part(p, p - 1))
                back[2 * f, f] = v
                back[2 * f + 1, f, 0] = gamma
        hi, lo = np_split(send)
        rows = np.concatenate([hi, lo], axis=1)
        sends.append(np.concatenate([rows, rows], axis=2))
        hi, lo = np_split(back.reshape(16, 4 * cells))
        backs.append(np.concatenate([hi, hi, lo, lo], axis=0))
    return np.stack(mats), np.stack(sends), np.stack(backs)


def halves(a):
    hi = a.astype(bf16)
    return hi, (a - hi.astype(f32)).astype(bf16)


def dot(a, b, dims=((1,), (0,))):
    return lax.dot_general(a, b, (dims, ((), ())), preferred_element_type=f32)


def inner_kernel(
    u_ref, v_ref, w_ref, p_ref, amats, xcols, ymats, ysends, ybacks,
    ready, part, recvx, xcol,
    field, amat, ymat, ysend, yback, wsum, sendx, sendy, recvy,
    in_sem, con_sem, sx, rx, sy, ry, far,
):
    depth, rows, cells = u_ref.shape
    nx, ny = lax.axis_size("gx"), lax.axis_size("gy")
    ix, iy = lax.axis_index("gx"), lax.axis_index("gy")
    right, left = lax.rem(ix + 1, nx), lax.rem(ix + nx - 1, nx)
    up, down = lax.rem(iy + 1, ny), lax.rem(iy + ny - 1, ny)
    has_up, has_down = iy < ny - 1, iy > 0

    loads = [
        pltpu.make_async_copy(src, field.at[k], in_sem.at[k])
        for k, src in enumerate((u_ref, v_ref, w_ref, p_ref))
    ]
    consts = [
        pltpu.make_async_copy(src, dst, con_sem.at[k])
        for k, (src, dst) in enumerate(
            (
                (xcols.at[pl.ds(2, 2)], wsum),
                (ysends.at[iy], ysend),
                (ymats.at[iy], ymat),
                (amats, amat),
                (ybacks.at[iy], yback),
                (xcols, xcol),
            )
        )
    ]
    for c in consts[:1] + loads + consts[1:]:
        c.start()

    barrier = pltpu.get_barrier_semaphore()
    pl.semaphore_signal(barrier, inc=1, device_id={"gx": left}, device_id_type=MESH)

    @pl.when(ix < nx - 1)
    def _():
        pl.semaphore_signal(barrier, inc=1, device_id={"gx": right}, device_id_type=MESH)

    @pl.when(has_up)
    def _():
        pl.semaphore_signal(barrier, inc=1, device_id={"gy": up}, device_id_type=MESH)

    @pl.when(has_down)
    def _():
        pl.semaphore_signal(barrier, inc=1, device_id={"gy": down}, device_id_type=MESH)

    def copy_x(side, k):
        return pltpu.make_async_remote_copy(
            src_ref=sendx.at[side, k], dst_ref=recvx.at[side, k],
            send_sem=sx.at[side, k], recv_sem=rx.at[side, k],
            device_id={"gx": (right, left)[side]}, device_id_type=MESH,
        )

    def copy_y(side):
        return pltpu.make_async_remote_copy(
            src_ref=sendy.at[side], dst_ref=recvy.at[side],
            send_sem=sy.at[side], recv_sem=ry.at[side],
            device_id={"gy": (up, down)[side]}, device_id_type=MESH,
        )

    zeros = jnp.zeros(recvy.shape[1:], f32)

    @pl.when(jnp.logical_not(has_down))
    def _():
        recvy[0] = zeros

    @pl.when(jnp.logical_not(has_up))
    def _():
        recvy[1] = zeros

    across = 1 + lax.div(ix + nx - 1, nx)
    along = 1 - lax.div(iy + 1, ny) + lax.div(iy + ny - 1, ny)

    def enter():
        pl.semaphore_wait(barrier, across + along)

    def meet():
        @pl.when(ix == nx - 1)
        def _():
            pl.semaphore_signal(far, inc=1, device_id={"gx": right}, device_id_type=MESH)

    def sum_x(side, k):
        sendx[side, k, 0] = jnp.sum(field[k] * wsum[side][None], axis=1)
        sendx[side, k, 1] = field[k, :, (rows - 1, 0)[side], :]

    def sum_y():
        consts[1].wait()
        sums = None
        for k in range(4):
            hi, lo = halves(field[k].reshape(depth * rows, cells))
            term = dot(ysend[k], jnp.concatenate([hi, lo], axis=1), ((1,), (1,)))
            sums = term if sums is None else sums + term
        sums = sums[0:16] + sums[16:32]
        sendy[0] = sums[0:8]
        sendy[1] = sums[8:16]

    def send_y():
        @pl.when(has_up)
        def _():
            copy_y(0).start()

        @pl.when(has_down)
        def _():
            copy_y(1).start()

    def own(z, carry):
        planes = [field[k, z] for k in range(4)]
        split = [halves(a) for a in planes]
        wide = jnp.concatenate([jnp.concatenate(s, axis=1) for s in split], axis=0)
        both = dot(wide, ymat[...])
        dy = both[:, :cells] + both[:, cells:]
        dy = [dy[k * rows : (k + 1) * rows] for k in range(4)]
        tall = jnp.concatenate([jnp.concatenate(s + s, axis=0) for s in split], axis=1)
        dx = dot(amat[...], tall)
        dx = [dx[:, k * cells : (k + 1) * cells] for k in range(4)]

        def at(k, shift):
            return field[k, lax.rem(z + shift + depth, depth)]

        dz = [
            0.75 * (at(k, 1) - at(k, -1))
            - 0.15 * (at(k, 2) - at(k, -2))
            + (1.0 / 60.0) * (at(k, 3) - at(k, -3))
            for k in range(4)
        ]
        u, v, w, _ = planes
        jx = -dx[3] - field_by * w
        jy = -dy[3] + field_bx * w
        jz = -dz[3] + field_by * u - field_bx * v
        ready[0, z] = -field_by * jz
        ready[1, z] = field_bx * jz
        ready[2, z] = dy[2] - dz[1]
        part[0, z] = field_by * jx - field_bx * jy
        part[1, z] = dz[0] - dx[2]
        part[2, z] = dx[1] - dy[0]
        part[3, z] = dx[0] + dy[1] + dz[2]
        return carry

    def compute():
        consts[2].wait()
        consts[3].wait()
        lax.fori_loop(0, depth, own, 0, unroll=2)

    consts[0].wait()

    @pl.when(ix == 0)
    def _():
        for k in range(4):
            loads[k].wait()
            for side in range(2):
                sum_x(side, k)
        sum_y()
        enter()
        send_y()
        for k in range(4):
            copy_x(0, k).start()
        compute()
        pl.semaphore_wait(far, 1)
        for k in range(4):
            copy_x(1, k).start()

    @pl.when(ix != 0)
    def _():
        for side in range(2):
            for k in range(4):
                if side == 0:
                    loads[k].wait()
                sum_x(side, k)
                if side == 0 and k == 0:
                    enter()
                    meet()
                copy_x(side, k).start()
        sum_y()
        send_y()
        compute()

    consts[4].wait()

    @pl.when(has_up)
    def _():
        copy_y(0).wait_send()
        copy_y(1).wait_recv()

    @pl.when(has_down)
    def _():
        copy_y(1).wait_send()
        copy_y(0).wait_recv()

    span = 128 // rows

    def edges(g, carry):
        where = pl.ds(pl.multiple_of(g * 128, 128), 128)
        got = jnp.concatenate([recvy[0, :, where], recvy[1, :, where]], axis=0)
        hi, lo = halves(got)
        ty = dot(jnp.concatenate([hi, lo, hi, lo], axis=0), yback[...], ((0,), (0,)))
        for q in range(span):
            z = g * span + q
            ey = [
                ty[q * rows : (q + 1) * rows, k * cells : (k + 1) * cells] for k in range(4)
            ]
            ready[2, z] += ey[2]
            part[0, z] += field_bx * ey[3]
            part[2, z] -= ey[0]
            part[3, z] += ey[1]
        return carry

    lax.fori_loop(0, depth // span, edges, 0, unroll=4)
    consts[5].wait()
    for side in range(2):
        for k in range(4):
            copy_x(side, k).wait()


def outer_kernel(ready, part, recvx, xcol, lor, vor, div, done, sem):
    _, depth, rows, cells = part.shape
    through = [
        pltpu.make_async_copy(ready.at[pl.ds(0, 2)], lor.at[pl.ds(0, 2)], sem.at[4]),
        pltpu.make_async_copy(ready.at[2], vor.at[0], sem.at[5]),
    ]
    for c in through:
        c.start()
    plan = (
        (lor.at[2], 3, -field_by),
        (vor.at[1], 2, -1.0),
        (vor.at[2], 1, 1.0),
        (div, 0, 1.0),
    )
    span = 2

    def edges(g, carry):
        planes = pl.ds(g * span, span)
        for a, (target, k, factor) in enumerate(plan):
            for q in range(span):
                z = g * span + q
                lo_sum, lo_cell, hi_sum, hi_cell = [
                    factor * recvx[side, k, what, pl.ds(z, 1), :]
                    for side in range(2)
                    for what in range(2)
                ]
                e = part[a, z] + xcol[0] * lo_sum + xcol[1] * hi_sum
                top = e[:8] + xcol[4, :8] * lo_cell
                end = e[rows - 8 :] + xcol[5, rows - 8 :] * hi_cell
                done[a, z] = jnp.concatenate([top, e[8 : rows - 8], end], axis=0)
            pltpu.make_async_copy(done.at[a, planes], target.at[planes], sem.at[a]).start()
        return carry

    lax.fori_loop(0, depth // span, edges, 0)
    for a, (target, _, _) in enumerate(plan):
        pltpu.make_async_copy(done.at[a], target, sem.at[a]).wait()
    for c in through:
        c.wait()


def local(tables, velocity_u, velocity_v, velocity_w, potential):
    depth, rows, cells = velocity_u.shape
    amat, xcol, ymats, ysends, ybacks = tables
    vmem = pl.BlockSpec(memory_space=pltpu.VMEM)
    hbm = pl.BlockSpec(memory_space=pltpu.HBM)
    dma = pltpu.SemaphoreType.DMA

    def shape(*dims, dtype=f32):
        return jax.ShapeDtypeStruct(dims, dtype)

    inner = pl.pallas_call(
        inner_kernel,
        out_shape=(
            shape(3, depth, rows, cells),
            shape(4, depth, rows, cells),
            shape(2, 4, 2, depth, cells),
            shape(*xcol.shape),
        ),
        in_specs=[hbm] * 9,
        out_specs=[vmem] * 4,
        scratch_shapes=[
            pltpu.VMEM((4, depth, rows, cells), f32),
            pltpu.VMEM(amat.shape, bf16),
            pltpu.VMEM(ymats.shape[1:], bf16),
            pltpu.VMEM(ysends.shape[1:], bf16),
            pltpu.VMEM(ybacks.shape[1:], bf16),
            pltpu.VMEM((2, rows, cells), f32),
            pltpu.VMEM((2, 4, 2, depth, cells), f32),
            pltpu.VMEM((2, 8, depth * rows), f32),
            pltpu.VMEM((2, 8, depth * rows), f32),
            dma((4,)),
            dma((6,)),
            dma((2, 4)),
            dma((2, 4)),
            dma((2,)),
            dma((2,)),
            pltpu.SemaphoreType.REGULAR,
        ],
        compiler_params=pltpu.CompilerParams(
            collective_id=0, has_side_effects=True, vmem_limit_bytes=16 * 2**20
        ),
    )(
        *(
            pltpu.with_memory_space_constraint(a, pltpu.HBM)
            for a in (velocity_u, velocity_v, velocity_w, potential, *map(jnp.asarray, tables))
        )
    )
    return pl.pallas_call(
        outer_kernel,
        out_shape=(
            shape(3, depth, rows, cells),
            shape(3, depth, rows, cells),
            shape(depth, rows, cells),
        ),
        in_specs=[vmem] * 4,
        out_specs=[hbm] * 3,
        scratch_shapes=[pltpu.VMEM((4, depth, rows, cells), f32), dma((6,))],
        compiler_params=pltpu.CompilerParams(vmem_limit_bytes=16 * 2**20),
    )(*inner)


def solution(mesh):
    spec = P(None, "gx", "gy")
    wide = P(None, None, "gx", "gy")

    def whole(velocity_u, velocity_v, velocity_w, potential):
        _, total_x, total_y = velocity_u.shape
        rows, cells = total_x // mesh.shape["gx"], total_y // mesh.shape["gy"]
        tables = x_tables(rows, cells) + y_tables(cells, mesh.shape["gy"])
        return jax.shard_map(
            functools.partial(local, tables),
            mesh=mesh,
            in_specs=(spec,) * 4,
            out_specs=(wide, wide, spec),
            check_vma=False,
        )(velocity_u, velocity_v, velocity_w, potential)

    return whole
```

```python
import functools

import jax
import jax.numpy as jnp
import numpy as np
from jax import lax
from jax.experimental import pallas as pl
from jax.experimental.pallas import tpu as pltpu
from jax.sharding import PartitionSpec as P

alpha_inner = 1.0 / 3.0
coef_near = 7.0 / 9.0
coef_far = 1.0 / 36.0
field_bx = 0.6
field_by = 0.8
MESH = pl.DeviceIdType.MESH
f32 = jnp.float32
bf16 = jnp.bfloat16


def np_split(a):
    hi = a.astype(np.float32).astype(bf16)
    lo = (a - hi.astype(np.float64)).astype(np.float32).astype(bf16)
    return hi, lo


def green(offset):
    root = (-1.0 + np.sqrt(1.0 - 4.0 * alpha_inner**2)) / (2.0 * alpha_inner)
    peak = 1.0 / np.sqrt(1.0 - 4.0 * alpha_inner**2)

    def pulse(k):
        return peak * root ** np.abs(k).astype(np.float64)

    near = pulse(offset - 1) - pulse(offset + 1)
    far = pulse(offset - 2) - pulse(offset + 2)
    return coef_near * near + coef_far * far


def x_line(rows):
    i = np.arange(rows)[:, None]
    j = np.arange(-rows, 2 * rows)[None, :]
    whole = green(j - i)
    return whole[:, :rows], whole[:, rows : 2 * rows], whole[:, 2 * rows :]


def y_operator(total):
    t = np.eye(total) + alpha_inner * (np.eye(total, k=1) + np.eye(total, k=-1))
    b = coef_near * (np.eye(total, k=1) - np.eye(total, k=-1))
    b += coef_far * (np.eye(total, k=2) - np.eye(total, k=-2))
    for r, s in ((0, 1), (total - 1, -1)):
        t[r] = 0.0
        b[r] = 0.0
        t[r, r], t[r, r + s] = 1.0, 2.0
        b[r, r], b[r, r + s], b[r, r + 2 * s] = -2.5 * s, 2.0 * s, 0.5 * s
        q = r + s
        t[q] = 0.0
        b[q] = 0.0
        t[q, q - 1], t[q, q], t[q, q + 1] = 0.25, 1.0, 0.25
        b[q, q + 1], b[q, q - 1] = 0.75, -0.75
    return np.linalg.solve(t, b)


def from_left(block):
    v = block[:, -1].copy()
    s = block[1] / block[1, -1]
    v[0] = block[0, -2] / s[-2]
    return v, s, block[0, -1] - v[0]


def from_right(block):
    v, s, gamma = from_left(block[::-1, ::-1])
    return v[::-1], s[::-1], gamma


def x_tables(rows, lanes):
    left, own, right = x_line(rows)
    hi, lo = np_split(own)
    amat = np.concatenate([hi, hi, lo, lo], axis=1)
    vl, sl, gl = from_left(left)
    vr, sr, gr = from_right(right)
    first = np.zeros(rows)
    first[0] = gl
    last = np.zeros(rows)
    last[-1] = gr
    cols = np.stack([vl, vr, sl, sr, first, last])
    return amat, np.repeat(cols[:, :, None], lanes, axis=2).astype(np.float32)


def y_tables(cells, count):
    d = y_operator(cells * count)

    def part(p, q):
        return d[p * cells : (p + 1) * cells, q * cells : (q + 1) * cells]

    mats, sends, backs = [], [], []
    for p in range(count):
        hi, lo = np_split(part(p, p).T)
        mats.append(np.block([[hi, lo], [hi, lo]]))
        send = np.zeros((4, 16, cells))
        back = np.zeros((16, 4, cells))
        for f in range(4):
            if p + 1 < count:
                send[f, 2 * f] = from_left(part(p + 1, p))[1]
                send[f, 2 * f + 1, -1] = 1.0
                v, _, gamma = from_right(part(p, p + 1))
                back[8 + 2 * f, f] = v
                back[8 + 2 * f + 1, f, -1] = gamma
            if p > 0:
                send[f, 8 + 2 * f] = from_right(part(p - 1, p))[1]
                send[f, 8 + 2 * f + 1, 0] = 1.0
                v, _, gamma = from_left(part(p, p - 1))
                back[2 * f, f] = v
                back[2 * f + 1, f, 0] = gamma
        hi, lo = np_split(send)
        rows = np.concatenate([hi, lo], axis=1)
        sends.append(np.concatenate([rows, rows], axis=2))
        hi, lo = np_split(back.reshape(16, 4 * cells))
        backs.append(np.concatenate([hi, hi, lo, lo], axis=0))
    return np.stack(mats), np.stack(sends), np.stack(backs)


def halves(a):
    hi = a.astype(bf16)
    return hi, (a - hi.astype(f32)).astype(bf16)


def dot(a, b, dims=((1,), (0,))):
    return lax.dot_general(a, b, (dims, ((), ())), preferred_element_type=f32)


def inner_kernel(
    u_ref, v_ref, w_ref, p_ref, amats, xcols, ymats, ysends, ybacks,
    ready, part, recvx, xcol,
    field, amat, ymat, ysend, yback, wsum, sendx, sendy, recvy,
    in_sem, con_sem, sx, rx, sy, ry, far,
):
    depth, rows, cells = u_ref.shape
    nx, ny = lax.axis_size("gx"), lax.axis_size("gy")
    ix, iy = lax.axis_index("gx"), lax.axis_index("gy")
    right, left = lax.rem(ix + 1, nx), lax.rem(ix + nx - 1, nx)
    up, down = lax.rem(iy + 1, ny), lax.rem(iy + ny - 1, ny)
    has_up, has_down = iy < ny - 1, iy > 0

    sources = (u_ref, v_ref, w_ref, p_ref)
    loads = [
        pltpu.make_async_copy(src, field.at[k], in_sem.at[k]) for k, src in enumerate(sources)
    ]
    consts = [
        pltpu.make_async_copy(src, dst, con_sem.at[k])
        for k, (src, dst) in enumerate(
            (
                (xcols.at[pl.ds(2, 2)], wsum),
                (ysends.at[iy], ysend),
                (ymats.at[iy], ymat),
                (amats, amat),
                (ybacks.at[iy], yback),
                (xcols, xcol),
            )
        )
    ]
    for c in consts[:1] + loads + consts[1:]:
        c.start()

    barrier = pltpu.get_barrier_semaphore()
    pl.semaphore_signal(barrier, inc=1, device_id={"gx": left}, device_id_type=MESH)

    @pl.when(ix < nx - 1)
    def _():
        pl.semaphore_signal(barrier, inc=1, device_id={"gx": right}, device_id_type=MESH)

    @pl.when(has_up)
    def _():
        pl.semaphore_signal(barrier, inc=1, device_id={"gy": up}, device_id_type=MESH)

    @pl.when(has_down)
    def _():
        pl.semaphore_signal(barrier, inc=1, device_id={"gy": down}, device_id_type=MESH)

    def copy_x(side, k):
        return pltpu.make_async_remote_copy(
            src_ref=sendx.at[side, k], dst_ref=recvx.at[0, side, k],
            send_sem=sx.at[0, side, k], recv_sem=rx.at[0, side, k],
            device_id={"gx": (right, left)[side]}, device_id_type=MESH,
        )

    def copy_edge(side, k):
        return pltpu.make_async_remote_copy(
            src_ref=sources[k].at[:, (rows - 1, 0)[side], :], dst_ref=recvx.at[1, side, k],
            send_sem=sx.at[1, side, k], recv_sem=rx.at[1, side, k],
            device_id={"gx": (right, left)[side]}, device_id_type=MESH,
        )

    def copy_y(side):
        return pltpu.make_async_remote_copy(
            src_ref=sendy.at[side], dst_ref=recvy.at[side],
            send_sem=sy.at[side], recv_sem=ry.at[side],
            device_id={"gy": (up, down)[side]}, device_id_type=MESH,
        )

    zeros = jnp.zeros(recvy.shape[1:], f32)

    @pl.when(jnp.logical_not(has_down))
    def _():
        recvy[0] = zeros

    @pl.when(jnp.logical_not(has_up))
    def _():
        recvy[1] = zeros

    across = 1 + lax.div(ix + nx - 1, nx)
    along = 1 - lax.div(iy + 1, ny) + lax.div(iy + ny - 1, ny)

    def enter():
        pl.semaphore_wait(barrier, across + along)

    def meet():
        @pl.when(ix == nx - 1)
        def _():
            pl.semaphore_signal(far, inc=1, device_id={"gx": right}, device_id_type=MESH)

    def sum_x(side, k):
        sendx[side, k] = jnp.sum(field[k] * wsum[side][None], axis=1)

    def sum_y():
        consts[1].wait()
        sums = None
        for k in range(4):
            hi, lo = halves(field[k].reshape(depth * rows, cells))
            term = dot(ysend[k], jnp.concatenate([hi, lo], axis=1), ((1,), (1,)))
            sums = term if sums is None else sums + term
        sums = sums[0:16] + sums[16:32]
        sendy[0] = sums[0:8]
        sendy[1] = sums[8:16]

    def send_y():
        @pl.when(has_up)
        def _():
            copy_y(0).start()

        @pl.when(has_down)
        def _():
            copy_y(1).start()

    def own(z, carry):
        planes = [field[k, z] for k in range(4)]
        split = [halves(a) for a in planes]
        wide = jnp.concatenate([jnp.concatenate(s, axis=1) for s in split], axis=0)
        both = dot(wide, ymat[...])
        dy = both[:, :cells] + both[:, cells:]
        dy = [dy[k * rows : (k + 1) * rows] for k in range(4)]
        tall = jnp.concatenate([jnp.concatenate(s + s, axis=0) for s in split], axis=1)
        dx = dot(amat[...], tall)
        dx = [dx[:, k * cells : (k + 1) * cells] for k in range(4)]

        def at(k, shift):
            return field[k, lax.rem(z + shift + depth, depth)]

        dz = [
            0.75 * (at(k, 1) - at(k, -1))
            - 0.15 * (at(k, 2) - at(k, -2))
            + (1.0 / 60.0) * (at(k, 3) - at(k, -3))
            for k in range(4)
        ]
        u, v, w, _ = planes
        jx = -dx[3] - field_by * w
        jy = -dy[3] + field_bx * w
        jz = -dz[3] + field_by * u - field_bx * v
        ready[0, z] = -field_by * jz
        ready[1, z] = field_bx * jz
        ready[2, z] = dy[2] - dz[1]
        part[0, z] = field_by * jx - field_bx * jy
        part[1, z] = dz[0] - dx[2]
        part[2, z] = dx[1] - dy[0]
        part[3, z] = dx[0] + dy[1] + dz[2]
        return carry

    def compute():
        consts[2].wait()
        consts[3].wait()
        lax.fori_loop(0, depth, own, 0, unroll=2)

    @pl.when(ix == 0)
    def _():
        consts[0].wait()
        for k in range(4):
            loads[k].wait()
            for side in range(2):
                sum_x(side, k)
        sum_y()
        enter()
        send_y()
        for k in range(4):
            copy_edge(0, k).start()
            copy_x(0, k).start()
        compute()
        pl.semaphore_wait(far, 1)
        for k in range(4):
            copy_edge(1, k).start()
            copy_x(1, k).start()

    @pl.when(ix != 0)
    def _():
        enter()
        for k in range(4):
            copy_edge(0, k).start()
        meet()
        consts[0].wait()
        for side in range(2):
            for k in range(4):
                if side == 0:
                    loads[k].wait()
                sum_x(side, k)
                copy_x(side, k).start()
        for k in range(4):
            copy_edge(1, k).start()
        sum_y()
        send_y()
        compute()

    consts[4].wait()

    @pl.when(has_up)
    def _():
        copy_y(0).wait_send()
        copy_y(1).wait_recv()

    @pl.when(has_down)
    def _():
        copy_y(1).wait_send()
        copy_y(0).wait_recv()

    span = 128 // rows

    def edges(g, carry):
        where = pl.ds(pl.multiple_of(g * 128, 128), 128)
        got = jnp.concatenate([recvy[0, :, where], recvy[1, :, where]], axis=0)
        hi, lo = halves(got)
        ty = dot(jnp.concatenate([hi, lo, hi, lo], axis=0), yback[...], ((0,), (0,)))
        for q in range(span):
            z = g * span + q
            ey = [
                ty[q * rows : (q + 1) * rows, k * cells : (k + 1) * cells] for k in range(4)
            ]
            ready[2, z] += ey[2]
            part[0, z] += field_bx * ey[3]
            part[2, z] -= ey[0]
            part[3, z] += ey[1]
        return carry

    lax.fori_loop(0, depth // span, edges, 0, unroll=4)
    consts[5].wait()
    for side in range(2):
        for k in range(4):
            copy_x(side, k).wait()
            copy_edge(side, k).wait()


def outer_kernel(ready, part, recvx, xcol, lor, vor, div, done, sem):
    _, depth, rows, cells = part.shape
    through = [
        pltpu.make_async_copy(ready.at[pl.ds(0, 2)], lor.at[pl.ds(0, 2)], sem.at[4]),
        pltpu.make_async_copy(ready.at[2], vor.at[0], sem.at[5]),
    ]
    for c in through:
        c.start()
    plan = (
        (lor.at[2], 3, -field_by),
        (vor.at[1], 2, -1.0),
        (vor.at[2], 1, 1.0),
        (div, 0, 1.0),
    )
    span = 2

    def edges(g, carry):
        planes = pl.ds(g * span, span)
        for a, (target, k, factor) in enumerate(plan):
            for q in range(span):
                z = g * span + q
                lo_sum, lo_cell, hi_sum, hi_cell = [
                    factor * recvx[what, side, k, pl.ds(z, 1), :]
                    for side in range(2)
                    for what in range(2)
                ]
                e = part[a, z] + xcol[0] * lo_sum + xcol[1] * hi_sum
                top = e[:8] + xcol[4, :8] * lo_cell
                end = e[rows - 8 :] + xcol[5, rows - 8 :] * hi_cell
                done[a, z] = jnp.concatenate([top, e[8 : rows - 8], end], axis=0)
            pltpu.make_async_copy(done.at[a, planes], target.at[planes], sem.at[a]).start()
        return carry

    lax.fori_loop(0, depth // span, edges, 0)
    for a, (target, _, _) in enumerate(plan):
        pltpu.make_async_copy(done.at[a], target, sem.at[a]).wait()
    for c in through:
        c.wait()


def local(tables, velocity_u, velocity_v, velocity_w, potential):
    depth, rows, cells = velocity_u.shape
    amat, xcol, ymats, ysends, ybacks = tables
    vmem = pl.BlockSpec(memory_space=pltpu.VMEM)
    hbm = pl.BlockSpec(memory_space=pltpu.HBM)
    dma = pltpu.SemaphoreType.DMA

    def shape(*dims, dtype=f32):
        return jax.ShapeDtypeStruct(dims, dtype)

    inner = pl.pallas_call(
        inner_kernel,
        out_shape=(
            shape(3, depth, rows, cells),
            shape(4, depth, rows, cells),
            shape(2, 2, 4, depth, cells),
            shape(*xcol.shape),
        ),
        in_specs=[hbm] * 9,
        out_specs=[vmem] * 4,
        scratch_shapes=[
            pltpu.VMEM((4, depth, rows, cells), f32),
            pltpu.VMEM(amat.shape, bf16),
            pltpu.VMEM(ymats.shape[1:], bf16),
            pltpu.VMEM(ysends.shape[1:], bf16),
            pltpu.VMEM(ybacks.shape[1:], bf16),
            pltpu.VMEM((2, rows, cells), f32),
            pltpu.VMEM((2, 4, depth, cells), f32),
            pltpu.VMEM((2, 8, depth * rows), f32),
            pltpu.VMEM((2, 8, depth * rows), f32),
            dma((4,)),
            dma((6,)),
            dma((2, 2, 4)),
            dma((2, 2, 4)),
            dma((2,)),
            dma((2,)),
            pltpu.SemaphoreType.REGULAR,
        ],
        compiler_params=pltpu.CompilerParams(
            collective_id=0, has_side_effects=True, vmem_limit_bytes=16 * 2**20
        ),
    )(
        *(
            pltpu.with_memory_space_constraint(a, pltpu.HBM)
            for a in (velocity_u, velocity_v, velocity_w, potential, *map(jnp.asarray, tables))
        )
    )
    return pl.pallas_call(
        outer_kernel,
        out_shape=(
            shape(3, depth, rows, cells),
            shape(3, depth, rows, cells),
            shape(depth, rows, cells),
        ),
        in_specs=[vmem] * 4,
        out_specs=[hbm] * 3,
        scratch_shapes=[pltpu.VMEM((4, depth, rows, cells), f32), dma((6,))],
        compiler_params=pltpu.CompilerParams(vmem_limit_bytes=16 * 2**20),
    )(*inner)


def solution(mesh):
    spec = P(None, "gx", "gy")
    wide = P(None, None, "gx", "gy")

    def whole(velocity_u, velocity_v, velocity_w, potential):
        _, total_x, total_y = velocity_u.shape
        rows, cells = total_x // mesh.shape["gx"], total_y // mesh.shape["gy"]
        tables = x_tables(rows, cells) + y_tables(cells, mesh.shape["gy"])
        return jax.shard_map(
            functools.partial(local, tables),
            mesh=mesh,
            in_specs=(spec,) * 4,
            out_specs=(wide, wide, spec),
            check_vma=False,
        )(velocity_u, velocity_v, velocity_w, potential)

    return whole
```

```python
import functools

import jax
import jax.numpy as jnp
import numpy as np
from jax import lax
from jax.experimental import pallas as pl
from jax.experimental.pallas import tpu as pltpu
from jax.sharding import PartitionSpec as P

alpha_inner = 1.0 / 3.0
coef_near = 7.0 / 9.0
coef_far = 1.0 / 36.0
field_bx = 0.6
field_by = 0.8
MESH = pl.DeviceIdType.MESH
f32 = jnp.float32
bf16 = jnp.bfloat16


def np_split(a):
    hi = a.astype(np.float32).astype(bf16)
    lo = (a - hi.astype(np.float64)).astype(np.float32).astype(bf16)
    return hi, lo


def green(offset):
    root = (-1.0 + np.sqrt(1.0 - 4.0 * alpha_inner**2)) / (2.0 * alpha_inner)
    peak = 1.0 / np.sqrt(1.0 - 4.0 * alpha_inner**2)

    def pulse(k):
        return peak * root ** np.abs(k).astype(np.float64)

    near = pulse(offset - 1) - pulse(offset + 1)
    far = pulse(offset - 2) - pulse(offset + 2)
    return coef_near * near + coef_far * far


def x_line(rows):
    i = np.arange(rows)[:, None]
    j = np.arange(-rows, 2 * rows)[None, :]
    whole = green(j - i)
    return whole[:, :rows], whole[:, rows : 2 * rows], whole[:, 2 * rows :]


def y_operator(total):
    t = np.eye(total) + alpha_inner * (np.eye(total, k=1) + np.eye(total, k=-1))
    b = coef_near * (np.eye(total, k=1) - np.eye(total, k=-1))
    b += coef_far * (np.eye(total, k=2) - np.eye(total, k=-2))
    for r, s in ((0, 1), (total - 1, -1)):
        t[r] = 0.0
        b[r] = 0.0
        t[r, r], t[r, r + s] = 1.0, 2.0
        b[r, r], b[r, r + s], b[r, r + 2 * s] = -2.5 * s, 2.0 * s, 0.5 * s
        q = r + s
        t[q] = 0.0
        b[q] = 0.0
        t[q, q - 1], t[q, q], t[q, q + 1] = 0.25, 1.0, 0.25
        b[q, q + 1], b[q, q - 1] = 0.75, -0.75
    return np.linalg.solve(t, b)


def from_left(block):
    v = block[:, -1].copy()
    s = block[1] / block[1, -1]
    v[0] = block[0, -2] / s[-2]
    return v, s, block[0, -1] - v[0]


def from_right(block):
    v, s, gamma = from_left(block[::-1, ::-1])
    return v[::-1], s[::-1], gamma


def x_tables(rows, lanes):
    left, own, right = x_line(rows)
    hi, lo = np_split(own)
    amat = np.concatenate([hi, hi, lo, lo], axis=1)
    vl, sl, gl = from_left(left)
    vr, sr, gr = from_right(right)
    first = np.zeros(rows)
    first[0] = gl
    last = np.zeros(rows)
    last[-1] = gr
    cols = np.stack([vl, vr, sl, sr, first, last])
    return amat, np.repeat(cols[:, :, None], lanes, axis=2).astype(np.float32)


def y_tables(cells, count):
    d = y_operator(cells * count)

    def part(p, q):
        return d[p * cells : (p + 1) * cells, q * cells : (q + 1) * cells]

    mats, sends, backs = [], [], []
    for p in range(count):
        hi, lo = np_split(part(p, p).T)
        mats.append(np.block([[hi, lo], [hi, lo]]))
        send = np.zeros((4, 16, cells))
        back = np.zeros((16, 4, cells))
        for f in range(4):
            if p + 1 < count:
                send[f, 2 * f] = from_left(part(p + 1, p))[1]
                send[f, 2 * f + 1, -1] = 1.0
                v, _, gamma = from_right(part(p, p + 1))
                back[8 + 2 * f, f] = v
                back[8 + 2 * f + 1, f, -1] = gamma
            if p > 0:
                send[f, 8 + 2 * f] = from_right(part(p - 1, p))[1]
                send[f, 8 + 2 * f + 1, 0] = 1.0
                v, _, gamma = from_left(part(p, p - 1))
                back[2 * f, f] = v
                back[2 * f + 1, f, 0] = gamma
        hi, lo = np_split(send)
        rows = np.concatenate([hi, lo], axis=1)
        sends.append(np.concatenate([rows, rows], axis=2))
        hi, lo = np_split(back.reshape(16, 4 * cells))
        backs.append(np.concatenate([hi, hi, lo, lo], axis=0))
    return np.stack(mats), np.stack(sends), np.stack(backs)


def halves(a):
    hi = a.astype(bf16)
    return hi, (a - hi.astype(f32)).astype(bf16)


def dot(a, b, dims=((1,), (0,))):
    return lax.dot_general(a, b, (dims, ((), ())), preferred_element_type=f32)


def inner_kernel(
    u_ref, v_ref, w_ref, p_ref, amats, xcols, ymats, ysends, ybacks,
    ready, part, recvx, xcol,
    field, amat, ymat, ysend, yback, wsum, sendx, sendy, recvy,
    in_sem, con_sem, sx, rx, sy, ry, far,
):
    depth, rows, cells = u_ref.shape
    nx, ny = lax.axis_size("gx"), lax.axis_size("gy")
    ix, iy = lax.axis_index("gx"), lax.axis_index("gy")
    right, left = lax.rem(ix + 1, nx), lax.rem(ix + nx - 1, nx)
    up, down = lax.rem(iy + 1, ny), lax.rem(iy + ny - 1, ny)
    has_up, has_down = iy < ny - 1, iy > 0

    sources = (u_ref, v_ref, w_ref, p_ref)
    loads = [
        pltpu.make_async_copy(src, field.at[k], in_sem.at[k]) for k, src in enumerate(sources)
    ]
    consts = [
        pltpu.make_async_copy(src, dst, con_sem.at[k])
        for k, (src, dst) in enumerate(
            (
                (xcols.at[pl.ds(2, 2)], wsum),
                (ysends.at[iy], ysend),
                (ymats.at[iy], ymat),
                (amats, amat),
                (ybacks.at[iy], yback),
                (xcols, xcol),
            )
        )
    ]
    for c in consts[:1] + loads:
        c.start()

    def start_tables():
        for c in consts[1:]:
            c.start()

    barrier = pltpu.get_barrier_semaphore()
    pl.semaphore_signal(barrier, inc=1, device_id={"gx": left}, device_id_type=MESH)

    @pl.when(ix < nx - 1)
    def _():
        pl.semaphore_signal(barrier, inc=1, device_id={"gx": right}, device_id_type=MESH)

    @pl.when(has_up)
    def _():
        pl.semaphore_signal(barrier, inc=1, device_id={"gy": up}, device_id_type=MESH)

    @pl.when(has_down)
    def _():
        pl.semaphore_signal(barrier, inc=1, device_id={"gy": down}, device_id_type=MESH)

    def copy_x(side, k):
        return pltpu.make_async_remote_copy(
            src_ref=sendx.at[side, k], dst_ref=recvx.at[0, side, k],
            send_sem=sx.at[0, side, k], recv_sem=rx.at[0, side, k],
            device_id={"gx": (right, left)[side]}, device_id_type=MESH,
        )

    def copy_edge(side, k):
        return pltpu.make_async_remote_copy(
            src_ref=sources[k].at[:, (rows - 1, 0)[side], :], dst_ref=recvx.at[1, side, k],
            send_sem=sx.at[1, side, k], recv_sem=rx.at[1, side, k],
            device_id={"gx": (right, left)[side]}, device_id_type=MESH,
        )

    def copy_y(side):
        return pltpu.make_async_remote_copy(
            src_ref=sendy.at[side], dst_ref=recvy.at[side],
            send_sem=sy.at[side], recv_sem=ry.at[side],
            device_id={"gy": (up, down)[side]}, device_id_type=MESH,
        )

    zeros = jnp.zeros(recvy.shape[1:], f32)

    @pl.when(jnp.logical_not(has_down))
    def _():
        recvy[0] = zeros

    @pl.when(jnp.logical_not(has_up))
    def _():
        recvy[1] = zeros

    across = 1 + lax.div(ix + nx - 1, nx)
    along = 1 - lax.div(iy + 1, ny) + lax.div(iy + ny - 1, ny)

    def enter():
        pl.semaphore_wait(barrier, across + along)

    def meet():
        @pl.when(ix == nx - 1)
        def _():
            pl.semaphore_signal(far, inc=1, device_id={"gx": right}, device_id_type=MESH)

    def sum_x(side, k):
        sendx[side, k] = jnp.sum(field[k] * wsum[side][None], axis=1)

    def sum_y():
        consts[1].wait()
        sums = None
        for k in range(4):
            hi, lo = halves(field[k].reshape(depth * rows, cells))
            term = dot(ysend[k], jnp.concatenate([hi, lo], axis=1), ((1,), (1,)))
            sums = term if sums is None else sums + term
        sums = sums[0:16] + sums[16:32]
        sendy[0] = sums[0:8]
        sendy[1] = sums[8:16]

    def send_y():
        @pl.when(has_up)
        def _():
            copy_y(0).start()

        @pl.when(has_down)
        def _():
            copy_y(1).start()

    def own(z, carry):
        planes = [field[k, z] for k in range(4)]
        split = [halves(a) for a in planes]
        wide = jnp.concatenate([jnp.concatenate(s, axis=1) for s in split], axis=0)
        both = dot(wide, ymat[...])
        dy = both[:, :cells] + both[:, cells:]
        dy = [dy[k * rows : (k + 1) * rows] for k in range(4)]
        tall = jnp.concatenate([jnp.concatenate(s + s, axis=0) for s in split], axis=1)
        dx = dot(amat[...], tall)
        dx = [dx[:, k * cells : (k + 1) * cells] for k in range(4)]

        def at(k, shift):
            return field[k, lax.rem(z + shift + depth, depth)]

        dz = [
            0.75 * (at(k, 1) - at(k, -1))
            - 0.15 * (at(k, 2) - at(k, -2))
            + (1.0 / 60.0) * (at(k, 3) - at(k, -3))
            for k in range(4)
        ]
        u, v, w, _ = planes
        jx = -dx[3] - field_by * w
        jy = -dy[3] + field_bx * w
        jz = -dz[3] + field_by * u - field_bx * v
        ready[0, z] = -field_by * jz
        ready[1, z] = field_bx * jz
        ready[2, z] = dy[2] - dz[1]
        part[0, z] = field_by * jx - field_bx * jy
        part[1, z] = dz[0] - dx[2]
        part[2, z] = dx[1] - dy[0]
        part[3, z] = dx[0] + dy[1] + dz[2]
        return carry

    def compute():
        consts[2].wait()
        consts[3].wait()
        lax.fori_loop(0, depth, own, 0, unroll=2)

    @pl.when(ix == 0)
    def _():
        start_tables()
        consts[0].wait()
        for k in range(4):
            loads[k].wait()
            for side in range(2):
                sum_x(side, k)
        sum_y()
        enter()
        send_y()
        for k in range(4):
            copy_edge(0, k).start()
            copy_x(0, k).start()
        compute()
        pl.semaphore_wait(far, 1)
        for k in range(4):
            copy_edge(1, k).start()
            copy_x(1, k).start()

    @pl.when(ix != 0)
    def _():
        enter()
        for k in range(4):
            copy_edge(0, k).start()
        meet()
        consts[0].wait()
        for side in range(2):
            for k in range(4):
                if side == 0:
                    loads[k].wait()
                sum_x(side, k)
                copy_x(side, k).start()
            if side == 0:
                start_tables()
        for k in range(4):
            copy_edge(1, k).start()
        sum_y()
        send_y()
        compute()

    consts[4].wait()

    @pl.when(has_up)
    def _():
        copy_y(0).wait_send()
        copy_y(1).wait_recv()

    @pl.when(has_down)
    def _():
        copy_y(1).wait_send()
        copy_y(0).wait_recv()

    span = 128 // rows

    def edges(g, carry):
        where = pl.ds(pl.multiple_of(g * 128, 128), 128)
        got = jnp.concatenate([recvy[0, :, where], recvy[1, :, where]], axis=0)
        hi, lo = halves(got)
        ty = dot(jnp.concatenate([hi, lo, hi, lo], axis=0), yback[...], ((0,), (0,)))
        for q in range(span):
            z = g * span + q
            ey = [
                ty[q * rows : (q + 1) * rows, k * cells : (k + 1) * cells] for k in range(4)
            ]
            ready[2, z] += ey[2]
            part[0, z] += field_bx * ey[3]
            part[2, z] -= ey[0]
            part[3, z] += ey[1]
        return carry

    lax.fori_loop(0, depth // span, edges, 0, unroll=4)
    consts[5].wait()
    for side in range(2):
        for k in range(4):
            copy_x(side, k).wait()
            copy_edge(side, k).wait()


def outer_kernel(ready, part, recvx, xcol, lor, vor, div, done, sem):
    _, depth, rows, cells = part.shape
    through = [
        pltpu.make_async_copy(ready.at[pl.ds(0, 2)], lor.at[pl.ds(0, 2)], sem.at[4]),
        pltpu.make_async_copy(ready.at[2], vor.at[0], sem.at[5]),
    ]
    for c in through:
        c.start()
    plan = (
        (lor.at[2], 3, -field_by),
        (vor.at[1], 2, -1.0),
        (vor.at[2], 1, 1.0),
        (div, 0, 1.0),
    )
    span = 2

    def edges(g, carry):
        planes = pl.ds(g * span, span)
        for a, (target, k, factor) in enumerate(plan):
            for q in range(span):
                z = g * span + q
                lo_sum, lo_cell, hi_sum, hi_cell = [
                    factor * recvx[what, side, k, pl.ds(z, 1), :]
                    for side in range(2)
                    for what in range(2)
                ]
                e = part[a, z] + xcol[0] * lo_sum + xcol[1] * hi_sum
                top = e[:8] + xcol[4, :8] * lo_cell
                end = e[rows - 8 :] + xcol[5, rows - 8 :] * hi_cell
                done[a, z] = jnp.concatenate([top, e[8 : rows - 8], end], axis=0)
            pltpu.make_async_copy(done.at[a, planes], target.at[planes], sem.at[a]).start()
        return carry

    lax.fori_loop(0, depth // span, edges, 0)
    for a, (target, _, _) in enumerate(plan):
        pltpu.make_async_copy(done.at[a], target, sem.at[a]).wait()
    for c in through:
        c.wait()


def local(tables, velocity_u, velocity_v, velocity_w, potential):
    depth, rows, cells = velocity_u.shape
    amat, xcol, ymats, ysends, ybacks = tables
    vmem = pl.BlockSpec(memory_space=pltpu.VMEM)
    hbm = pl.BlockSpec(memory_space=pltpu.HBM)
    dma = pltpu.SemaphoreType.DMA

    def shape(*dims, dtype=f32):
        return jax.ShapeDtypeStruct(dims, dtype)

    inner = pl.pallas_call(
        inner_kernel,
        out_shape=(
            shape(3, depth, rows, cells),
            shape(4, depth, rows, cells),
            shape(2, 2, 4, depth, cells),
            shape(*xcol.shape),
        ),
        in_specs=[hbm] * 9,
        out_specs=[vmem] * 4,
        scratch_shapes=[
            pltpu.VMEM((4, depth, rows, cells), f32),
            pltpu.VMEM(amat.shape, bf16),
            pltpu.VMEM(ymats.shape[1:], bf16),
            pltpu.VMEM(ysends.shape[1:], bf16),
            pltpu.VMEM(ybacks.shape[1:], bf16),
            pltpu.VMEM((2, rows, cells), f32),
            pltpu.VMEM((2, 4, depth, cells), f32),
            pltpu.VMEM((2, 8, depth * rows), f32),
            pltpu.VMEM((2, 8, depth * rows), f32),
            dma((4,)),
            dma((6,)),
            dma((2, 2, 4)),
            dma((2, 2, 4)),
            dma((2,)),
            dma((2,)),
            pltpu.SemaphoreType.REGULAR,
        ],
        compiler_params=pltpu.CompilerParams(
            collective_id=0, has_side_effects=True, vmem_limit_bytes=16 * 2**20
        ),
    )(
        *(
            pltpu.with_memory_space_constraint(a, pltpu.HBM)
            for a in (velocity_u, velocity_v, velocity_w, potential, *map(jnp.asarray, tables))
        )
    )
    return pl.pallas_call(
        outer_kernel,
        out_shape=(
            shape(3, depth, rows, cells),
            shape(3, depth, rows, cells),
            shape(depth, rows, cells),
        ),
        in_specs=[vmem] * 4,
        out_specs=[hbm] * 3,
        scratch_shapes=[pltpu.VMEM((4, depth, rows, cells), f32), dma((6,))],
        compiler_params=pltpu.CompilerParams(vmem_limit_bytes=16 * 2**20),
    )(*inner)


def solution(mesh):
    spec = P(None, "gx", "gy")
    wide = P(None, None, "gx", "gy")

    def whole(velocity_u, velocity_v, velocity_w, potential):
        _, total_x, total_y = velocity_u.shape
        rows, cells = total_x // mesh.shape["gx"], total_y // mesh.shape["gy"]
        tables = x_tables(rows, cells) + y_tables(cells, mesh.shape["gy"])
        return jax.shard_map(
            functools.partial(local, tables),
            mesh=mesh,
            in_specs=(spec,) * 4,
            out_specs=(wide, wide, spec),
            check_vma=False,
        )(velocity_u, velocity_v, velocity_w, potential)

    return whole
```
